32 devices in a mesh: grp: 4 (over y, x), fsdp: 8 (over z, core).
Axes of the slice: x: 2, y: 2, z: 4, core: 2. Of those that a mesh axis runs over, the one named last changes fastest.
Arguments:
- tokens: bfloat16 [64, 4096], P(('grp', 'fsdp')), may hold values from -128 to 128
- norm_gain: float32 [4096], replicated, may hold values from 0.25 to 1.75
- routes: int32 [64, 8], P(('grp', 'fsdp')), may hold values from 0 to 31, all different within a row; in each aligned block of 16 rows (0 to 15, 16 to 31, ...) at most 8 rows name the same one
- gate_probs: bfloat16 [64, 8], P(('grp', 'fsdp')), may hold values from 0.019897461 to 1
- w_gate_up: bfloat16 [32, 4096, 2048], P(('grp', 'fsdp')), may hold values from -0.09375 to 0.09375
- w_down: bfloat16 [32, 1024, 4096], P(('grp', 'fsdp')), may hold values from -0.1875 to 0.1875
Outputs:
- moe_out: bfloat16 [64, 4096], P(('grp', 'fsdp'))
The draws below stay inside these ranges and needn't reach their ends.
Inputs may be any that keep to these rules, and one draw needn't show every extreme that they name: `routes`: each row names 8 different experts. In every aligned block of 16 rows no expert is named by more than 8 rows, a bound that some block reaches.
All inputs are finite; a program needn't handle non-finite values.
Results may differ from the reference program's by a relative error of at most 0.0095.
Values may be sent and summed in bfloat16 or wider, within the bound.
No kernel may reach another device: no remote copies, remote signals or barrier semaphores. Data moves between devices by JAX's collectives and lax.ppermute only.
A program may use at most 64 MiB of HBM per device.

```python
import math
import jax
import jax.numpy as jnp
import numpy as np
from jax import lax

D = 4096
FF = 1024
TOPK = 8
ROWS = 64
FSPLIT = 1
EXPERTS = 32
FF_DEV = 1024
SLICES = 32
BLOCK = 16
CAP = 8
N_GRP = 4


def draw_tokens(key, part):
    key_base, key_rows, key_cols = jax.random.split(key, 3)
    base_values = jnp.clip(jax.random.normal(key_base, (ROWS, D), jnp.float32), -4.0, 4.0)
    row_scale = jnp.exp(jax.random.uniform(key_rows, (ROWS, 1), jnp.float32, 0.0, math.log(10.0)))
    col_scale = jnp.exp(jax.random.uniform(key_cols, (1, D), jnp.float32, math.log(0.5), math.log(2.0)))
    return (base_values * row_scale * col_scale).astype(jnp.bfloat16)


def block_scale(key, shape, pieces, smallest, top_value):
    def one(position, shards_of):
        steps = jax.random.uniform(jax.random.fold_in(jax.random.fold_in(key, 6), position), (shards_of,), jnp.float32, smallest / len(pieces), top_value / len(pieces))
        return jnp.repeat(jnp.exp(steps), shape[position] // shards_of).reshape((-1,) + (1,) * (len(shape) - position - 1))

    level = one(*pieces[0])
    for cut in pieces[1:]:
        level = level * one(*cut)
    return level


def assign_block(key, own, number, rows, number_of, top, reach, skew):
    ranking = jax.random.permutation(key, number_of)
    packed, usual = portions_of(number_of, rows * top, reach, skew, True), portions_of(number_of, rows * top, reach, skew, False)
    places = jnp.arange(number_of)

    def named(lengths, rotation):
        used = int((lengths > 0).sum())
        fixed = max(1, used // 4)
        passed = fixed + (places - fixed + rotation * (used - fixed)) % max(1, number_of - fixed)
        return jnp.zeros((number_of,), jnp.int32).at[ranking[jnp.where(places < fixed, places, passed)]].set(jnp.asarray(lengths, jnp.int32))

    lengths = jnp.where(number % 4 == 0, named(packed, number // 4), named(usual, number - number // 4 - 1))
    mixed = jax.random.permutation(jax.random.fold_in(own, 3), number_of)
    source_of, receiver = mixed[0:number_of // 2 * 2:2], mixed[1:number_of // 2 * 2:2]
    margin = jnp.minimum(lengths[source_of] - 1, reach - lengths[receiver]) // 2
    margin = jnp.where((source_of == ranking[0]) | (receiver == ranking[0]) | (lengths[receiver] == 0), 0, jnp.maximum(margin, 0))
    passed = jax.random.randint(jax.random.fold_in(own, 4), (number_of // 2,), 0, 1 << 20) % (margin + 1)
    lengths = lengths.at[source_of].add(-passed).at[receiver].add(passed)
    labels = jnp.searchsorted(jnp.cumsum(lengths), jnp.arange(rows * top), side="right").astype(jnp.int32)
    table = labels.reshape(top, rows).T
    table = table[jax.random.permutation(jax.random.fold_in(own, 1), rows)]
    rotation = jax.random.randint(jax.random.fold_in(own, 2), (rows, 1), 0, top)
    return jnp.take_along_axis(table, (jnp.arange(top)[None, :] + rotation) % top, axis=1)


def portions_of(number_of, total, reach, lean, full):
    loads = [(1 << 20) // math.isqrt(grade ** lean) + 1 for grade in range(1, number_of + 1)]
    largest = reach if full else min(reach, max(-(-total // number_of), total * loads[0] // sum(loads)))
    least = 1 if total - largest >= number_of - 1 else 0
    given, rest = [largest] + [least] * (number_of - 1), total - largest - least * (number_of - 1)
    while rest > 0:
        free = [i for i in range(1, number_of) if given[i] < largest] or [i for i in range(1, number_of) if given[i] < reach]
        mass, remaining = sum([loads[i] for i in free]), rest
        for i in free:
            addition = min(reach - given[i], max(1, remaining * loads[i] // mass), rest)
            given[i] = given[i] + addition
            rest = rest - addition
    return np.array(given)


def bell_draw(own_key, extent, deviation, most, cuts=(), kind=jnp.bfloat16):
    values = deviation * jax.random.normal(own_key, extent, jnp.float32)
    if cuts:
        values = values * block_scale(own_key, extent, cuts, -0.22, 0.18)
    return jnp.clip(values, -most, most).astype(kind)


def setup_inputs(seed: int = 0) -> dict:
    key_of = jax.random.split(jax.random.key(seed), 7)
    tokens = draw_tokens(jax.random.fold_in(key_of[6], 71), 0)
    norm_gain = jnp.clip(1.0 + 0.15 * jax.random.normal(key_of[1], (D,), jnp.float32), 0.25, 1.75)
    routes_keys = jax.random.split(jax.random.fold_in(key_of[2], 1), ROWS // BLOCK)
    routes_turns = jax.random.permutation(jax.random.fold_in(key_of[2], 3), ROWS // BLOCK)
    routes = jax.vmap(lambda own, number: assign_block(jax.random.fold_in(key_of[2], 2), own, number, BLOCK, EXPERTS, TOPK, CAP, 2))(routes_keys, routes_turns).reshape((ROWS, TOPK))
    gate_probs = jnp.clip(jnp.exp(math.log(1.0) - 3.9171631 * jax.random.uniform(key_of[3], (ROWS, TOPK), jnp.float32) ** block_scale(key_of[3], (ROWS, TOPK), ((0, 32),), -0.2, 0.2)), 0.019897461, 1.0).astype(jnp.bfloat16)
    w_gate_up = bell_draw(key_of[4], (SLICES, D, 2 * FF_DEV), D ** -0.5, 0.09375, ((0, 32),))
    w_down = bell_draw(key_of[5], (SLICES, FF_DEV, D), FF ** -0.5, 0.1875, ((0, 32),))
    return dict(tokens=tokens, norm_gain=norm_gain, routes=routes, gate_probs=gate_probs, w_gate_up=w_gate_up, w_down=w_down)


def reference(tokens, norm_gain, routes, gate_probs, w_gate_up, w_down):
    as_float = tokens.astype(jnp.float32)
    mean_square = lax.optimization_barrier(jnp.mean(as_float * as_float, axis=-1, keepdims=True))
    normed = (as_float * lax.rsqrt(mean_square + 1e-06) * norm_gain).astype(jnp.bfloat16)
    probs = gate_probs.astype(jnp.float32)
    combine = probs / lax.optimization_barrier(jnp.sum(probs, axis=-1, keepdims=True))
    row_ids = jnp.arange(ROWS, dtype=jnp.int32)
    picked_count = N_GRP * CAP

    def one_expert(expert, summed):
        matched = routes == expert
        is_routed = jnp.any(matched, axis=1)
        row_weight = lax.optimization_barrier(jnp.sum(jnp.where(matched, combine, 0.0), axis=1))
        sort_key = jnp.where(is_routed, row_ids, row_ids + ROWS).astype(jnp.int32)
        order = jnp.argsort(sort_key)[:picked_count].astype(jnp.int32)
        picked = normed[order].astype(jnp.float32)
        weight_sel = jnp.where(is_routed[order], row_weight[order], 0.0)
        start = (expert * FSPLIT).astype(jnp.int32)
        gate_up = lax.dynamic_slice_in_dim(w_gate_up, start, FSPLIT, 0).astype(jnp.float32)
        down = lax.dynamic_slice_in_dim(w_down, start, FSPLIT, 0).astype(jnp.float32)
        projected = jnp.einsum('md,sdf->smf', picked, gate_up)
        hidden = (jax.nn.silu(projected[..., :FF_DEV]) * projected[..., FF_DEV:]).astype(jnp.bfloat16)
        result = jnp.einsum('smf,sfd->smd', hidden.astype(jnp.float32), down).astype(jnp.bfloat16)
        contrib = lax.optimization_barrier(jnp.sum(weight_sel[None, :, None] * result.astype(jnp.float32), axis=0))
        return summed.at[order].add(contrib)
    summed = lax.fori_loop(0, EXPERTS, one_expert, jnp.zeros((ROWS, D), jnp.float32))
    return summed.astype(jnp.bfloat16)
```

```python
import jax
import jax.numpy as jnp
from jax import lax
from jax.sharding import PartitionSpec as P

FF = 1024
LANES = 128
AXES = ("grp", "fsdp")


def rms_normed(tokens, norm_gain):
    as_float = tokens.astype(jnp.float32)
    mean_square = jnp.mean(as_float * as_float, axis=-1, keepdims=True)
    return (as_float * lax.rsqrt(mean_square + 1e-06) * norm_gain).astype(jnp.bfloat16)


def expert_mlp(rows, w_gate_up, w_down):
    hidden_dev = w_down.shape[1]
    projected = jnp.dot(rows, w_gate_up[0], preferred_element_type=jnp.float32)
    hidden = (jax.nn.silu(projected[:, :hidden_dev]) * projected[:, hidden_dev:]).astype(
        jnp.bfloat16
    )
    return jnp.dot(hidden, w_down[0], preferred_element_type=jnp.float32).astype(jnp.bfloat16)


def every_row(tokens, norm_gain, routes, gate_probs, w_gate_up, w_down):
    device_count = lax.axis_size(AXES)
    pair_count = device_count // 2
    me = lax.axis_index(AXES)
    my_expert = me // (FF // w_down.shape[1])
    rows_dev, width = tokens.shape
    top_count = routes.shape[1]
    same_core = [[d for d in range(device_count) if d % 2 == k] for k in range(2)]
    partner = [(d, d ^ 1) for d in range(device_count)]

    normed = rms_normed(tokens, norm_gain)
    padding = jnp.zeros((rows_dev, -2 * top_count % LANES), jnp.bfloat16)
    payload = jnp.concatenate(
        [normed, routes.astype(jnp.bfloat16), gate_probs, padding], axis=1
    )
    outgoing = jnp.broadcast_to(payload[None], (pair_count,) + payload.shape)
    own = lax.all_to_all(outgoing, AXES, 0, 0, axis_index_groups=same_core, tiled=True)
    other = lax.ppermute(own, AXES, partner)
    rows = jnp.concatenate([own, other]).reshape(-1, payload.shape[1])

    sent_routes = rows[:, width : width + top_count].astype(jnp.int32)
    probs = rows[:, width + top_count : width + 2 * top_count].astype(jnp.float32)
    combine = probs / jnp.sum(probs, axis=-1, keepdims=True)
    row_weight = jnp.sum(jnp.where(sent_routes == my_expert, combine, 0.0), axis=-1)

    part = expert_mlp(rows[:, :width], w_gate_up, w_down)
    weighted = (part.astype(jnp.float32) * row_weight[:, None]).reshape(
        2, pair_count, rows_dev, width
    )
    from_partner = lax.ppermute(weighted[1].astype(jnp.bfloat16), AXES, partner)
    chip_sum = (weighted[0] + from_partner.astype(jnp.float32)).astype(jnp.bfloat16)
    returned = lax.all_to_all(chip_sum, AXES, 0, 0, axis_index_groups=same_core, tiled=True)
    return jnp.sum(returned.astype(jnp.float32), axis=0).astype(jnp.bfloat16)


def routed_rows(tokens, norm_gain, routes, gate_probs, w_gate_up, w_down):
    group_count = lax.axis_size("grp")
    shard_count = lax.axis_size("fsdp")
    shard_index = lax.axis_index("fsdp")
    split_count = FF // w_down.shape[1]
    rows_dev, width = tokens.shape
    block_rows = rows_dev * shard_count
    capacity = slot_capacity(tokens, routes, w_down)
    normed = rms_normed(tokens, norm_gain)
    rows_all = lax.all_gather(normed, "fsdp", axis=0, tiled=True)
    probs_all = lax.all_gather(gate_probs, "fsdp", axis=0, tiled=True)
    routes_all = lax.all_gather(routes, "fsdp", axis=0, tiled=True)
    probs = probs_all.astype(jnp.float32)
    combine = probs / jnp.sum(probs, axis=-1, keepdims=True)
    targets = (
        jnp.arange(group_count, dtype=jnp.int32) * (shard_count // split_count)
        + shard_index // split_count
    )
    matched = routes_all[None, :, :] == targets[:, None, None]
    is_routed = jnp.any(matched, axis=-1)
    row_weight = jnp.sum(jnp.where(matched, combine[None, :, :], 0.0), axis=-1)
    row_ids = jnp.arange(block_rows, dtype=jnp.int32)
    earlier = row_ids[:, None] >= row_ids[None, :]
    slot_index = jnp.sum(is_routed[:, None, :] & earlier[None], axis=-1, dtype=jnp.int32) - 1
    select = (
        slot_index[:, None, :] == jnp.arange(capacity, dtype=jnp.int32)[None, :, None]
    ) & is_routed[:, None, :]
    outgoing = jnp.einsum(
        "gcb,bd->gcd", select.astype(jnp.bfloat16), rows_all, preferred_element_type=jnp.float32
    ).astype(jnp.bfloat16)
    incoming = lax.all_to_all(outgoing, "grp", split_axis=0, concat_axis=0, tiled=True)
    result = expert_mlp(incoming.reshape(-1, width), w_gate_up, w_down)
    returned = lax.all_to_all(
        result.reshape(incoming.shape), "grp", split_axis=0, concat_axis=0, tiled=True
    )
    mix_matrix = (select.astype(jnp.float32) * row_weight[:, None, :]).reshape(-1, block_rows)
    row_partial = jnp.dot(
        mix_matrix.T,
        returned.reshape(-1, width),
        precision=lax.Precision.HIGHEST,
        preferred_element_type=jnp.float32,
    )
    summed = lax.psum_scatter(row_partial, "fsdp", scatter_dimension=0, tiled=True)
    return summed.astype(jnp.bfloat16)


def slot_capacity(tokens, routes, w_down):
    block_rows = tokens.shape[0] * lax.axis_size("fsdp")
    expert_count = lax.axis_size(AXES) * w_down.shape[1] // FF
    return 2 * block_rows * routes.shape[1] // expert_count


def local(tokens, norm_gain, routes, gate_probs, w_gate_up, w_down):
    block_rows = tokens.shape[0] * lax.axis_size("fsdp")
    dense = block_rows <= 2 * slot_capacity(tokens, routes, w_down)
    plan = every_row if dense and lax.axis_size("fsdp") % 2 == 0 else routed_rows
    return plan(tokens, norm_gain, routes, gate_probs, w_gate_up, w_down)


def solution(mesh):
    return jax.shard_map(
        local,
        mesh=mesh,
        in_specs=(
            P(AXES, None),
            P(),
            P(AXES, None),
            P(AXES, None),
            P(AXES, None, None),
            P(AXES, None, None),
        ),
        out_specs=P(AXES, None),
        check_vma=False,
    )
```

```python
import jax
import jax.numpy as jnp
from jax import lax
from jax.experimental import pallas as pl
from jax.experimental.pallas import tpu as pltpu
from jax.sharding import PartitionSpec as P

FF = 1024
LANES = 128
SMALL_VMEM = 2 << 20
MLP_VMEM = 24 << 20
AXES = ("grp", "fsdp")


def device_index():
    return lax.axis_index("grp") * lax.axis_size("fsdp") + lax.axis_index("fsdp")


def rms_normed(tokens, norm_gain):
    as_float = tokens.astype(jnp.float32)
    mean_square = jnp.mean(as_float * as_float, axis=-1, keepdims=True)
    return (as_float * lax.rsqrt(mean_square + 1e-06) * norm_gain).astype(jnp.bfloat16)


def expert_mlp(rows, w_gate_up, w_down):
    hidden_dev = w_down.shape[1]
    projected = jnp.dot(rows, w_gate_up[0], preferred_element_type=jnp.float32)
    hidden = (jax.nn.silu(projected[:, :hidden_dev]) * projected[:, hidden_dev:]).astype(
        jnp.bfloat16
    )
    return jnp.dot(hidden, w_down[0], preferred_element_type=jnp.float32).astype(jnp.bfloat16)


def row_payload(tokens, norm_gain, routes, gate_probs):
    rows_dev, width = tokens.shape
    top_count = routes.shape[1]
    total = width + LANES * -(-2 * top_count // LANES)

    def kernel(*refs):
        sources, payload_ref, targets, sems = refs[:4], refs[4], refs[5:9], refs[9]
        copies = [
            pltpu.make_async_copy(source, target, sems.at[index])
            for index, (source, target) in enumerate(zip(sources, targets))
        ]
        for copy in copies:
            copy.start()
        for copy in copies:
            copy.wait()
        tokens_ref, gain_ref, routes_ref, probs_ref = targets
        as_float = tokens_ref[...].astype(jnp.float32)
        mean_square = jnp.mean(as_float * as_float, axis=-1, keepdims=True)
        scaled = as_float * lax.rsqrt(mean_square + 1e-06) * gain_ref[...]
        payload_ref[:, :width] = scaled.astype(jnp.bfloat16)
        control = jnp.concatenate(
            [
                routes_ref[...].astype(jnp.float32),
                probs_ref[...].astype(jnp.float32),
                jnp.zeros((rows_dev, total - width - 2 * top_count), jnp.float32),
            ],
            axis=1,
        )
        payload_ref[:, width:] = control.astype(jnp.bfloat16)

    operands = (tokens, norm_gain.reshape(1, width), routes, gate_probs)
    return pl.pallas_call(
        kernel,
        out_shape=jax.ShapeDtypeStruct((rows_dev, total), jnp.bfloat16),
        in_specs=[pl.BlockSpec(memory_space=pltpu.HBM)] * 4,
        out_specs=pl.BlockSpec(memory_space=pltpu.VMEM),
        scratch_shapes=[pltpu.VMEM(o.shape, o.dtype) for o in operands]
        + [pltpu.SemaphoreType.DMA((4,))],
        compiler_params=pltpu.CompilerParams(vmem_limit_bytes=SMALL_VMEM),
        name="row_payload",
    )(*[pltpu.with_memory_space_constraint(o, pltpu.HBM) for o in operands])


def load_rows(weight, first, count, chunk_count=8):
    step = count // chunk_count

    def kernel(source, target, sems):
        copies = [
            pltpu.make_async_copy(
                source.at[0, pl.ds(first + chunk * step, step)],
                target.at[pl.ds(chunk * step, step)],
                sems.at[chunk],
            )
            for chunk in range(chunk_count)
        ]
        for copy in copies:
            copy.start()
        for copy in copies:
            copy.wait()

    shape = (count, weight.shape[2])
    return pl.pallas_call(
        kernel,
        out_shape=pltpu.VMEM(shape, weight.dtype),
        in_specs=[pl.BlockSpec(memory_space=pltpu.HBM)],
        out_specs=pl.BlockSpec(memory_space=pltpu.VMEM),
        scratch_shapes=[pltpu.SemaphoreType.DMA((chunk_count,))],
        compiler_params=pltpu.CompilerParams(vmem_limit_bytes=SMALL_VMEM),
        cost_estimate=pl.CostEstimate(
            flops=0, transcendentals=0, bytes_accessed=2 * count * weight.shape[2]
        ),
        name="load_rows",
    )(pltpu.with_memory_space_constraint(weight, pltpu.HBM))


def stacked(pieces):
    def kernel(*refs):
        for index, ref in enumerate(refs[:-1]):
            refs[-1][index] = ref[...]

    vmem = pl.BlockSpec(memory_space=pltpu.VMEM)
    return pl.pallas_call(
        kernel,
        out_shape=jax.ShapeDtypeStruct((len(pieces),) + pieces[0].shape, pieces[0].dtype),
        in_specs=[vmem] * len(pieces),
        out_specs=vmem,
        compiler_params=pltpu.CompilerParams(vmem_limit_bytes=SMALL_VMEM),
        name="stacked",
    )(*pieces)


def weighted_parts(own, other, gate_up_pieces, w_down, top_count):
    hidden_dev, width = w_down.shape[1:]
    blocks = list(own) + list(other)
    block_rows = blocks[0].shape[0] * blocks[0].shape[1]
    total = blocks[0].shape[2]
    row_count = block_rows * len(blocks)
    half = row_count // 2
    piece_count = len(gate_up_pieces)
    out_block = (half // blocks[0].shape[1], blocks[0].shape[1], width)

    def kernel(*refs):
        my_expert = device_index() // (FF // hidden_dev)
        block_refs, refs = refs[: len(blocks)], refs[len(blocks) :]
        piece_refs, refs = refs[:piece_count], refs[piece_count:]
        down_hbm, own_out, other_out, rows_ref, down_ref, sem = refs
        fetch = pltpu.make_async_copy(down_hbm.at[0], down_ref, sem)
        fetch.start()
        for index, source in enumerate(block_refs):
            rows_ref[index * block_rows : (index + 1) * block_rows, :] = source[...].reshape(
                block_rows, total
            )
        control = rows_ref[:, width:].astype(jnp.float32)
        sent_routes = control[:, :top_count].astype(jnp.int32)
        probs = control[:, top_count : 2 * top_count]
        combine = probs / jnp.sum(probs, axis=-1, keepdims=True)
        row_weight = jnp.sum(
            jnp.where(sent_routes == my_expert, combine, 0.0), axis=-1, keepdims=True
        )
        projected, first = None, 0
        for piece in piece_refs:
            last = first + piece.shape[0]
            term = jnp.dot(rows_ref[:, first:last], piece[...], preferred_element_type=jnp.float32)
            projected, first = term if projected is None else projected + term, last
        gate, up = projected[:, :hidden_dev], projected[:, hidden_dev:]
        hidden = (jax.nn.silu(gate) * up).astype(jnp.bfloat16)
        fetch.wait()
        part = jnp.dot(hidden, down_ref[...], preferred_element_type=jnp.float32)
        weighted = part.astype(jnp.bfloat16).astype(jnp.float32) * row_weight
        own_out[...] = weighted[:half].reshape(out_block)
        other_out[...] = weighted[half:].reshape(out_block).astype(jnp.bfloat16)

    vmem = pl.BlockSpec(memory_space=pltpu.VMEM)
    return pl.pallas_call(
        kernel,
        out_shape=[
            jax.ShapeDtypeStruct(out_block, jnp.float32),
            jax.ShapeDtypeStruct(out_block, jnp.bfloat16),
        ],
        in_specs=[vmem] * (len(blocks) + piece_count)
        + [pl.BlockSpec(memory_space=pltpu.HBM)],
        out_specs=[vmem] * 2,
        scratch_shapes=[
            pltpu.VMEM((row_count, total), jnp.bfloat16),
            pltpu.VMEM(w_down.shape[1:], w_down.dtype),
            pltpu.SemaphoreType.DMA,
        ],
        compiler_params=pltpu.CompilerParams(vmem_limit_bytes=MLP_VMEM),
        name="weighted_parts",
    )(
        *blocks,
        *[pltpu.with_memory_space_constraint(piece, pltpu.VMEM) for piece in gate_up_pieces],
        pltpu.with_memory_space_constraint(w_down, pltpu.HBM),
    )


def chip_sum(own_part, partner_part):
    pair_count = own_part.shape[0]

    def kernel(own_ref, partner_ref, sum_ref):
        my_chip = device_index() // 2
        for chip in range(pair_count):
            slot = jnp.bitwise_xor(my_chip, chip)
            total = own_ref[slot] + partner_ref[slot].astype(jnp.float32)
            sum_ref[chip] = total.astype(jnp.bfloat16)

    vmem = pl.BlockSpec(memory_space=pltpu.VMEM)
    return pl.pallas_call(
        kernel,
        out_shape=jax.ShapeDtypeStruct(own_part.shape, jnp.bfloat16),
        in_specs=[vmem] * 2,
        out_specs=vmem,
        compiler_params=pltpu.CompilerParams(vmem_limit_bytes=SMALL_VMEM),
        name="chip_sum",
    )(own_part, partner_part)


def exchanged(value, axis, flip):
    size = lax.axis_size(axis)
    return lax.ppermute(value, axis, [(d, d ^ flip) for d in range(size)])


def every_row(tokens, norm_gain, routes, gate_probs, w_gate_up, w_down):
    device_count = lax.axis_size(AXES)
    shard_count = lax.axis_size("fsdp")
    group_count = lax.axis_size("grp")
    same_core = [[d for d in range(device_count) if d % 2 == k] for k in range(2)]
    depth = w_gate_up.shape[1] // 2

    payload = row_payload(tokens, norm_gain, routes, gate_probs)
    column = [payload] + [exchanged(payload, "fsdp", k) for k in range(2, shard_count, 2)]
    column, first = lax.optimization_barrier((column, load_rows(w_gate_up, 0, depth)))
    column = stacked(column)
    plane = [exchanged(column, "grp", k) for k in range(1, group_count)]
    plane, second = lax.optimization_barrier((plane, load_rows(w_gate_up, depth, depth)))
    own = [column] + plane
    other = [exchanged(block, "fsdp", 1) for block in own]
    own_part, other_part = weighted_parts(own, other, [first, second], w_down, routes.shape[1])
    from_partner = exchanged(other_part, "fsdp", 1)
    summed = chip_sum(own_part, from_partner)
    returned = lax.all_to_all(summed, AXES, 0, 0, axis_index_groups=same_core, tiled=True)
    return jnp.sum(returned.astype(jnp.float32), axis=0).astype(jnp.bfloat16)


def routed_rows(tokens, norm_gain, routes, gate_probs, w_gate_up, w_down):
    group_count = lax.axis_size("grp")
    shard_count = lax.axis_size("fsdp")
    shard_index = lax.axis_index("fsdp")
    split_count = FF // w_down.shape[1]
    rows_dev, width = tokens.shape
    block_rows = rows_dev * shard_count
    capacity = slot_capacity(tokens, routes, w_down)
    normed = rms_normed(tokens, norm_gain)
    rows_all = lax.all_gather(normed, "fsdp", axis=0, tiled=True)
    probs_all = lax.all_gather(gate_probs, "fsdp", axis=0, tiled=True)
    routes_all = lax.all_gather(routes, "fsdp", axis=0, tiled=True)
    probs = probs_all.astype(jnp.float32)
    combine = probs / jnp.sum(probs, axis=-1, keepdims=True)
    targets = (
        jnp.arange(group_count, dtype=jnp.int32) * (shard_count // split_count)
        + shard_index // split_count
    )
    matched = routes_all[None, :, :] == targets[:, None, None]
    is_routed = jnp.any(matched, axis=-1)
    row_weight = jnp.sum(jnp.where(matched, combine[None, :, :], 0.0), axis=-1)
    row_ids = jnp.arange(block_rows, dtype=jnp.int32)
    earlier = row_ids[:, None] >= row_ids[None, :]
    slot_index = jnp.sum(is_routed[:, None, :] & earlier[None], axis=-1, dtype=jnp.int32) - 1
    select = (
        slot_index[:, None, :] == jnp.arange(capacity, dtype=jnp.int32)[None, :, None]
    ) & is_routed[:, None, :]
    outgoing = jnp.einsum(
        "gcb,bd->gcd", select.astype(jnp.bfloat16), rows_all, preferred_element_type=jnp.float32
    ).astype(jnp.bfloat16)
    incoming = lax.all_to_all(outgoing, "grp", split_axis=0, concat_axis=0, tiled=True)
    result = expert_mlp(incoming.reshape(-1, width), w_gate_up, w_down)
    returned = lax.all_to_all(
        result.reshape(incoming.shape), "grp", split_axis=0, concat_axis=0, tiled=True
    )
    mix_matrix = (select.astype(jnp.float32) * row_weight[:, None, :]).reshape(-1, block_rows)
    row_partial = jnp.dot(
        mix_matrix.T,
        returned.reshape(-1, width),
        precision=lax.Precision.HIGHEST,
        preferred_element_type=jnp.float32,
    )
    summed = lax.psum_scatter(row_partial, "fsdp", scatter_dimension=0, tiled=True)
    return summed.astype(jnp.bfloat16)


def slot_capacity(tokens, routes, w_down):
    block_rows = tokens.shape[0] * lax.axis_size("fsdp")
    expert_count = lax.axis_size(AXES) * w_down.shape[1] // FF
    return 2 * block_rows * routes.shape[1] // expert_count


def local(tokens, norm_gain, routes, gate_probs, w_gate_up, w_down):
    block_rows = tokens.shape[0] * lax.axis_size("fsdp")
    dense = block_rows <= 2 * slot_capacity(tokens, routes, w_down)
    paired = lax.axis_size("fsdp") > 1 and lax.axis_size(AXES) & (lax.axis_size(AXES) - 1) == 0
    plan = every_row if dense and paired else routed_rows
    return plan(tokens, norm_gain, routes, gate_probs, w_gate_up, w_down)


def solution(mesh):
    return jax.shard_map(
        local,
        mesh=mesh,
        in_specs=(
            P(AXES, None),
            P(),
            P(AXES, None),
            P(AXES, None),
            P(AXES, None, None),
            P(AXES, None, None),
        ),
        out_specs=P(AXES, None),
        check_vma=False,
    )
```

```python
import math

import jax
import jax.numpy as jnp
from jax import lax
from jax.experimental import pallas as pl
from jax.experimental.pallas import tpu as pltpu
from jax.sharding import PartitionSpec as P

FF = 1024
LANES = 128
SMALL_VMEM = 2 << 20
MLP_VMEM = 24 << 20
MLP_TILE = 512
AXES = ("grp", "fsdp")


def device_index():
    return lax.axis_index("grp") * lax.axis_size("fsdp") + lax.axis_index("fsdp")


def rms_normed(tokens, norm_gain):
    as_float = tokens.astype(jnp.float32)
    mean_square = jnp.mean(as_float * as_float, axis=-1, keepdims=True)
    return (as_float * lax.rsqrt(mean_square + 1e-06) * norm_gain).astype(jnp.bfloat16)


def expert_mlp(rows, w_gate_up, w_down):
    hidden_dev = w_down.shape[1]
    projected = jnp.dot(rows, w_gate_up[0], preferred_element_type=jnp.float32)
    hidden = (jax.nn.silu(projected[:, :hidden_dev]) * projected[:, hidden_dev:]).astype(
        jnp.bfloat16
    )
    return jnp.dot(hidden, w_down[0], preferred_element_type=jnp.float32).astype(jnp.bfloat16)


def row_payload(tokens, norm_gain, routes, gate_probs):
    rows_dev, width = tokens.shape
    top_count = routes.shape[1]
    total = width + LANES * -(-2 * top_count // LANES)

    def kernel(*refs):
        sources, payload_ref, targets, sems = refs[:4], refs[4], refs[5:9], refs[9]
        copies = [
            pltpu.make_async_copy(source, target, sems.at[index])
            for index, (source, target) in enumerate(zip(sources, targets))
        ]
        for copy in copies:
            copy.start()
        for copy in copies:
            copy.wait()
        tokens_ref, gain_ref, routes_ref, probs_ref = targets
        as_float = tokens_ref[...].astype(jnp.float32)
        mean_square = jnp.mean(as_float * as_float, axis=-1, keepdims=True)
        scaled = as_float * lax.rsqrt(mean_square + 1e-06) * gain_ref[...]
        payload_ref[:, :width] = scaled.astype(jnp.bfloat16)
        control = jnp.concatenate(
            [
                routes_ref[...].astype(jnp.float32),
                probs_ref[...].astype(jnp.float32),
                jnp.zeros((rows_dev, total - width - 2 * top_count), jnp.float32),
            ],
            axis=1,
        )
        payload_ref[:, width:] = control.astype(jnp.bfloat16)

    operands = (tokens, norm_gain.reshape(1, width), routes, gate_probs)
    return pl.pallas_call(
        kernel,
        out_shape=jax.ShapeDtypeStruct((rows_dev, total), jnp.bfloat16),
        in_specs=[pl.BlockSpec(memory_space=pltpu.HBM)] * 4,
        out_specs=pl.BlockSpec(memory_space=pltpu.VMEM),
        scratch_shapes=[pltpu.VMEM(o.shape, o.dtype) for o in operands]
        + [pltpu.SemaphoreType.DMA((4,))],
        compiler_params=pltpu.CompilerParams(vmem_limit_bytes=SMALL_VMEM),
        name="row_payload",
    )(*[pltpu.with_memory_space_constraint(o, pltpu.HBM) for o in operands])


def load_rows(weight, first, count, chunk_count=8):
    step = count // chunk_count

    def kernel(source, target, sems):
        copies = [
            pltpu.make_async_copy(
                source.at[0, pl.ds(first + chunk * step, step)],
                target.at[pl.ds(chunk * step, step)],
                sems.at[chunk],
            )
            for chunk in range(chunk_count)
        ]
        for copy in copies:
            copy.start()
        for copy in copies:
            copy.wait()

    shape = (count, weight.shape[2])
    return pl.pallas_call(
        kernel,
        out_shape=pltpu.VMEM(shape, weight.dtype),
        in_specs=[pl.BlockSpec(memory_space=pltpu.HBM)],
        out_specs=pl.BlockSpec(memory_space=pltpu.VMEM),
        scratch_shapes=[pltpu.SemaphoreType.DMA((chunk_count,))],
        compiler_params=pltpu.CompilerParams(vmem_limit_bytes=SMALL_VMEM),
        cost_estimate=pl.CostEstimate(
            flops=0, transcendentals=0, bytes_accessed=2 * count * weight.shape[2]
        ),
        name="load_rows",
    )(pltpu.with_memory_space_constraint(weight, pltpu.HBM))


def stacked(pieces):
    def kernel(*refs):
        for index, ref in enumerate(refs[:-1]):
            refs[-1][index] = ref[...]

    vmem = pl.BlockSpec(memory_space=pltpu.VMEM)
    return pl.pallas_call(
        kernel,
        out_shape=jax.ShapeDtypeStruct((len(pieces),) + pieces[0].shape, pieces[0].dtype),
        in_specs=[vmem] * len(pieces),
        out_specs=vmem,
        compiler_params=pltpu.CompilerParams(vmem_limit_bytes=SMALL_VMEM),
        name="stacked",
    )(*pieces)


def weighted_parts(own, other, gate_up_pieces, w_down, top_count):
    hidden_dev, width = w_down.shape[1:]
    blocks = list(own) + list(other)
    block_rows = blocks[0].shape[0] * blocks[0].shape[1]
    total = blocks[0].shape[2]
    row_count = block_rows * len(blocks)
    half = row_count // 2
    piece_count = len(gate_up_pieces)
    tile = math.gcd(math.gcd(hidden_dev, width), MLP_TILE)
    out_block = (half // blocks[0].shape[1], blocks[0].shape[1], width)

    def projected(rows_ref, piece_refs, column):
        sum_so_far, first = None, 0
        for piece in piece_refs:
            last = first + piece.shape[0]
            term = jnp.dot(
                rows_ref[:, first:last],
                piece[:, pl.ds(column, tile)],
                preferred_element_type=jnp.float32,
            )
            sum_so_far, first = term if sum_so_far is None else sum_so_far + term, last
        return sum_so_far

    def kernel(*refs):
        my_expert = device_index() // (FF // hidden_dev)
        block_refs, refs = refs[: len(blocks)], refs[len(blocks) :]
        piece_refs, refs = refs[:piece_count], refs[piece_count:]
        down_hbm, own_out, other_out, rows_ref, hidden_ref, down_ref, sem = refs
        fetch = pltpu.make_async_copy(down_hbm.at[0], down_ref, sem)
        fetch.start()
        for index, source in enumerate(block_refs):
            rows_ref[index * block_rows : (index + 1) * block_rows, :] = source[...].reshape(
                block_rows, total
            )
        control = rows_ref[:, width:].astype(jnp.float32)
        sent_routes = control[:, :top_count].astype(jnp.int32)
        probs = control[:, top_count : 2 * top_count]
        combine = probs / jnp.sum(probs, axis=-1, keepdims=True)
        row_weight = jnp.sum(
            jnp.where(sent_routes == my_expert, combine, 0.0), axis=-1, keepdims=True
        )
        @pl.loop(0, hidden_dev // tile)
        def _(step):
            column = pl.multiple_of(step * tile, tile)
            gate = projected(rows_ref, piece_refs, column)
            up = projected(rows_ref, piece_refs, pl.multiple_of(hidden_dev + column, tile))
            hidden_ref[:, pl.ds(column, tile)] = (jax.nn.silu(gate) * up).astype(jnp.bfloat16)

        fetch.wait()
        for column in range(0, width, tile):
            columns = slice(column, column + tile)
            part = jnp.dot(
                hidden_ref[...], down_ref[:, columns], preferred_element_type=jnp.float32
            )
            weighted = part.astype(jnp.bfloat16).astype(jnp.float32) * row_weight
            own_out[:, :, columns] = weighted[:half].reshape(out_block[:2] + (tile,))
            other_out[:, :, columns] = (
                weighted[half:].reshape(out_block[:2] + (tile,)).astype(jnp.bfloat16)
            )

    vmem = pl.BlockSpec(memory_space=pltpu.VMEM)
    return pl.pallas_call(
        kernel,
        out_shape=[
            jax.ShapeDtypeStruct(out_block, jnp.float32),
            jax.ShapeDtypeStruct(out_block, jnp.bfloat16),
        ],
        in_specs=[vmem] * (len(blocks) + piece_count)
        + [pl.BlockSpec(memory_space=pltpu.HBM)],
        out_specs=[vmem] * 2,
        scratch_shapes=[
            pltpu.VMEM((row_count, total), jnp.bfloat16),
            pltpu.VMEM((row_count, hidden_dev), jnp.bfloat16),
            pltpu.VMEM(w_down.shape[1:], w_down.dtype),
            pltpu.SemaphoreType.DMA,
        ],
        compiler_params=pltpu.CompilerParams(vmem_limit_bytes=MLP_VMEM),
        name="weighted_parts",
    )(
        *blocks,
        *[pltpu.with_memory_space_constraint(piece, pltpu.VMEM) for piece in gate_up_pieces],
        pltpu.with_memory_space_constraint(w_down, pltpu.HBM),
    )


def chip_sum(own_part, partner_part):
    pair_count = own_part.shape[0]

    def kernel(own_ref, partner_ref, sum_ref):
        my_chip = device_index() // 2
        for chip in range(pair_count):
            slot = jnp.bitwise_xor(my_chip, chip)
            total = own_ref[slot] + partner_ref[slot].astype(jnp.float32)
            sum_ref[chip] = total.astype(jnp.bfloat16)

    vmem = pl.BlockSpec(memory_space=pltpu.VMEM)
    return pl.pallas_call(
        kernel,
        out_shape=jax.ShapeDtypeStruct(own_part.shape, jnp.bfloat16),
        in_specs=[vmem] * 2,
        out_specs=vmem,
        compiler_params=pltpu.CompilerParams(vmem_limit_bytes=SMALL_VMEM),
        name="chip_sum",
    )(own_part, partner_part)


def exchanged(value, axis, flip):
    size = lax.axis_size(axis)
    return lax.ppermute(value, axis, [(d, d ^ flip) for d in range(size)])


def every_row(tokens, norm_gain, routes, gate_probs, w_gate_up, w_down):
    device_count = lax.axis_size(AXES)
    shard_count = lax.axis_size("fsdp")
    group_count = lax.axis_size("grp")
    same_core = [[d for d in range(device_count) if d % 2 == k] for k in range(2)]
    depth = w_gate_up.shape[1] // 2

    payload = row_payload(tokens, norm_gain, routes, gate_probs)
    column = [payload] + [exchanged(payload, "fsdp", k) for k in range(2, shard_count, 2)]
    column, first = lax.optimization_barrier((column, load_rows(w_gate_up, 0, depth)))
    column = stacked(column)
    plane = [exchanged(column, "grp", k) for k in range(1, group_count)]
    plane, second = lax.optimization_barrier((plane, load_rows(w_gate_up, depth, depth)))
    own = [column] + plane
    other = [exchanged(block, "fsdp", 1) for block in own]
    own_part, other_part = weighted_parts(own, other, [first, second], w_down, routes.shape[1])
    from_partner = exchanged(other_part, "fsdp", 1)
    summed = chip_sum(own_part, from_partner)
    returned = lax.all_to_all(summed, AXES, 0, 0, axis_index_groups=same_core, tiled=True)
    return jnp.sum(returned.astype(jnp.float32), axis=0).astype(jnp.bfloat16)


def routed_rows(tokens, norm_gain, routes, gate_probs, w_gate_up, w_down):
    group_count = lax.axis_size("grp")
    shard_count = lax.axis_size("fsdp")
    shard_index = lax.axis_index("fsdp")
    split_count = FF // w_down.shape[1]
    rows_dev, width = tokens.shape
    block_rows = rows_dev * shard_count
    capacity = slot_capacity(tokens, routes, w_down)
    normed = rms_normed(tokens, norm_gain)
    rows_all = lax.all_gather(normed, "fsdp", axis=0, tiled=True)
    probs_all = lax.all_gather(gate_probs, "fsdp", axis=0, tiled=True)
    routes_all = lax.all_gather(routes, "fsdp", axis=0, tiled=True)
    probs = probs_all.astype(jnp.float32)
    combine = probs / jnp.sum(probs, axis=-1, keepdims=True)
    targets = (
        jnp.arange(group_count, dtype=jnp.int32) * (shard_count // split_count)
        + shard_index // split_count
    )
    matched = routes_all[None, :, :] == targets[:, None, None]
    is_routed = jnp.any(matched, axis=-1)
    row_weight = jnp.sum(jnp.where(matched, combine[None, :, :], 0.0), axis=-1)
    row_ids = jnp.arange(block_rows, dtype=jnp.int32)
    earlier = row_ids[:, None] >= row_ids[None, :]
    slot_index = jnp.sum(is_routed[:, None, :] & earlier[None], axis=-1, dtype=jnp.int32) - 1
    select = (
        slot_index[:, None, :] == jnp.arange(capacity, dtype=jnp.int32)[None, :, None]
    ) & is_routed[:, None, :]
    outgoing = jnp.einsum(
        "gcb,bd->gcd", select.astype(jnp.bfloat16), rows_all, preferred_element_type=jnp.float32
    ).astype(jnp.bfloat16)
    incoming = lax.all_to_all(outgoing, "grp", split_axis=0, concat_axis=0, tiled=True)
    result = expert_mlp(incoming.reshape(-1, width), w_gate_up, w_down)
    returned = lax.all_to_all(
        result.reshape(incoming.shape), "grp", split_axis=0, concat_axis=0, tiled=True
    )
    mix_matrix = (select.astype(jnp.float32) * row_weight[:, None, :]).reshape(-1, block_rows)
    row_partial = jnp.dot(
        mix_matrix.T,
        returned.reshape(-1, width),
        precision=lax.Precision.HIGHEST,
        preferred_element_type=jnp.float32,
    )
    summed = lax.psum_scatter(row_partial, "fsdp", scatter_dimension=0, tiled=True)
    return summed.astype(jnp.bfloat16)


def slot_capacity(tokens, routes, w_down):
    block_rows = tokens.shape[0] * lax.axis_size("fsdp")
    expert_count = lax.axis_size(AXES) * w_down.shape[1] // FF
    return 2 * block_rows * routes.shape[1] // expert_count


def local(tokens, norm_gain, routes, gate_probs, w_gate_up, w_down):
    block_rows = tokens.shape[0] * lax.axis_size("fsdp")
    dense = block_rows <= 2 * slot_capacity(tokens, routes, w_down)
    paired = lax.axis_size("fsdp") > 1 and lax.axis_size(AXES) & (lax.axis_size(AXES) - 1) == 0
    plan = every_row if dense and paired else routed_rows
    return plan(tokens, norm_gain, routes, gate_probs, w_gate_up, w_down)


def solution(mesh):
    return jax.shard_map(
        local,
        mesh=mesh,
        in_specs=(
            P(AXES, None),
            P(),
            P(AXES, None),
            P(AXES, None),
            P(AXES, None, None),
            P(AXES, None, None),
        ),
        out_specs=P(AXES, None),
        check_vma=False,
    )
```

```python
import math

import jax
import jax.numpy as jnp
from jax import lax
from jax.experimental import pallas as pl
from jax.experimental.pallas import tpu as pltpu
from jax.sharding import PartitionSpec as P

FF = 1024
LANES = 128
SMALL_VMEM = 2 << 20
MLP_VMEM = 24 << 20
MLP_TILE = 512
PREFETCH_WINDOW = pl.CostEstimate(flops=64 << 30, transcendentals=0, bytes_accessed=256 << 20)
AXES = ("grp", "fsdp")


def device_index():
    return lax.axis_index("grp") * lax.axis_size("fsdp") + lax.axis_index("fsdp")


def rms_normed(tokens, norm_gain):
    as_float = tokens.astype(jnp.float32)
    mean_square = jnp.mean(as_float * as_float, axis=-1, keepdims=True)
    return (as_float * lax.rsqrt(mean_square + 1e-06) * norm_gain).astype(jnp.bfloat16)


def expert_mlp(rows, w_gate_up, w_down):
    hidden_dev = w_down.shape[1]
    projected = jnp.dot(rows, w_gate_up[0], preferred_element_type=jnp.float32)
    hidden = (jax.nn.silu(projected[:, :hidden_dev]) * projected[:, hidden_dev:]).astype(
        jnp.bfloat16
    )
    return jnp.dot(hidden, w_down[0], preferred_element_type=jnp.float32).astype(jnp.bfloat16)


def row_payload(tokens, norm_gain, routes, gate_probs):
    rows_dev, width = tokens.shape
    top_count = routes.shape[1]
    total = width + LANES * -(-2 * top_count // LANES)

    def kernel(*refs):
        sources, payload_ref, targets, sems = refs[:4], refs[4], refs[5:9], refs[9]
        copies = [
            pltpu.make_async_copy(source, target, sems.at[index])
            for index, (source, target) in enumerate(zip(sources, targets))
        ]
        for copy in copies:
            copy.start()
        for copy in copies:
            copy.wait()
        tokens_ref, gain_ref, routes_ref, probs_ref = targets
        as_float = tokens_ref[...].astype(jnp.float32)
        mean_square = jnp.mean(as_float * as_float, axis=-1, keepdims=True)
        scaled = as_float * lax.rsqrt(mean_square + 1e-06) * gain_ref[...]
        payload_ref[:, :width] = scaled.astype(jnp.bfloat16)
        control = jnp.concatenate(
            [
                routes_ref[...].astype(jnp.float32),
                probs_ref[...].astype(jnp.float32),
                jnp.zeros((rows_dev, total - width - 2 * top_count), jnp.float32),
            ],
            axis=1,
        )
        payload_ref[:, width:] = control.astype(jnp.bfloat16)

    operands = (tokens, norm_gain.reshape(1, width), routes, gate_probs)
    return pl.pallas_call(
        kernel,
        out_shape=jax.ShapeDtypeStruct((rows_dev, total), jnp.bfloat16),
        in_specs=[pl.BlockSpec(memory_space=pltpu.HBM)] * 4,
        out_specs=pl.BlockSpec(memory_space=pltpu.VMEM),
        scratch_shapes=[pltpu.VMEM(o.shape, o.dtype) for o in operands]
        + [pltpu.SemaphoreType.DMA((4,))],
        compiler_params=pltpu.CompilerParams(vmem_limit_bytes=SMALL_VMEM),
        name="row_payload",
    )(*[pltpu.with_memory_space_constraint(o, pltpu.HBM) for o in operands])


def stacked(pieces):
    def kernel(*refs):
        for index, ref in enumerate(refs[:-1]):
            refs[-1][index] = ref[...]

    vmem = pl.BlockSpec(memory_space=pltpu.VMEM)
    return pl.pallas_call(
        kernel,
        out_shape=jax.ShapeDtypeStruct((len(pieces),) + pieces[0].shape, pieces[0].dtype),
        in_specs=[vmem] * len(pieces),
        out_specs=vmem,
        compiler_params=pltpu.CompilerParams(vmem_limit_bytes=SMALL_VMEM),
        cost_estimate=PREFETCH_WINDOW,
        name="stacked",
    )(*pieces)


def weighted_parts(own, other, gate_up_pieces, w_down, top_count):
    hidden_dev, width = w_down.shape[1:]
    blocks = list(own) + list(other)
    block_rows = blocks[0].shape[0] * blocks[0].shape[1]
    total = blocks[0].shape[2]
    row_count = block_rows * len(blocks)
    half = row_count // 2
    piece_count = len(gate_up_pieces)
    tile = math.gcd(math.gcd(hidden_dev, width), MLP_TILE)
    out_block = (half // blocks[0].shape[1], blocks[0].shape[1], width)

    def projected(rows_ref, piece_refs, column):
        sum_so_far, first = None, 0
        for piece in piece_refs:
            last = first + piece.shape[0]
            term = jnp.dot(
                rows_ref[:, first:last],
                piece[:, pl.ds(column, tile)],
                preferred_element_type=jnp.float32,
            )
            sum_so_far, first = term if sum_so_far is None else sum_so_far + term, last
        return sum_so_far

    def kernel(*refs):
        my_expert = device_index() // (FF // hidden_dev)
        block_refs, refs = refs[: len(blocks)], refs[len(blocks) :]
        piece_refs, refs = refs[:piece_count], refs[piece_count:]
        down_hbm, own_out, other_out, rows_ref, hidden_ref, down_ref, sem = refs
        fetch = pltpu.make_async_copy(down_hbm.at[0], down_ref, sem)
        fetch.start()
        for index, source in enumerate(block_refs):
            rows_ref[index * block_rows : (index + 1) * block_rows, :] = source[...].reshape(
                block_rows, total
            )
        control = rows_ref[:, width:].astype(jnp.float32)
        sent_routes = control[:, :top_count].astype(jnp.int32)
        probs = control[:, top_count : 2 * top_count]
        combine = probs / jnp.sum(probs, axis=-1, keepdims=True)
        row_weight = jnp.sum(
            jnp.where(sent_routes == my_expert, combine, 0.0), axis=-1, keepdims=True
        )
        @pl.loop(0, hidden_dev // tile)
        def _(step):
            column = pl.multiple_of(step * tile, tile)
            gate = projected(rows_ref, piece_refs, column)
            up = projected(rows_ref, piece_refs, pl.multiple_of(hidden_dev + column, tile))
            hidden_ref[:, pl.ds(column, tile)] = (jax.nn.silu(gate) * up).astype(jnp.bfloat16)

        fetch.wait()
        for column in range(0, width, tile):
            columns = slice(column, column + tile)
            part = jnp.dot(
                hidden_ref[...], down_ref[:, columns], preferred_element_type=jnp.float32
            )
            weighted = part.astype(jnp.bfloat16).astype(jnp.float32) * row_weight
            own_out[:, :, columns] = weighted[:half].reshape(out_block[:2] + (tile,))
            other_out[:, :, columns] = (
                weighted[half:].reshape(out_block[:2] + (tile,)).astype(jnp.bfloat16)
            )

    vmem = pl.BlockSpec(memory_space=pltpu.VMEM)
    return pl.pallas_call(
        kernel,
        out_shape=[
            jax.ShapeDtypeStruct(out_block, jnp.float32),
            jax.ShapeDtypeStruct(out_block, jnp.bfloat16),
        ],
        in_specs=[vmem] * (len(blocks) + piece_count)
        + [pl.BlockSpec(memory_space=pltpu.HBM)],
        out_specs=[vmem] * 2,
        scratch_shapes=[
            pltpu.VMEM((row_count, total), jnp.bfloat16),
            pltpu.VMEM((row_count, hidden_dev), jnp.bfloat16),
            pltpu.VMEM(w_down.shape[1:], w_down.dtype),
            pltpu.SemaphoreType.DMA,
        ],
        compiler_params=pltpu.CompilerParams(vmem_limit_bytes=MLP_VMEM),
        name="weighted_parts",
    )(
        *blocks,
        *[pltpu.with_memory_space_constraint(piece, pltpu.VMEM) for piece in gate_up_pieces],
        pltpu.with_memory_space_constraint(w_down, pltpu.HBM),
    )


def chip_sum(own_part, partner_part):
    pair_count = own_part.shape[0]

    def kernel(own_ref, partner_ref, sum_ref):
        my_chip = device_index() // 2
        for chip in range(pair_count):
            slot = jnp.bitwise_xor(my_chip, chip)
            total = own_ref[slot] + partner_ref[slot].astype(jnp.float32)
            sum_ref[chip] = total.astype(jnp.bfloat16)

    vmem = pl.BlockSpec(memory_space=pltpu.VMEM)
    return pl.pallas_call(
        kernel,
        out_shape=jax.ShapeDtypeStruct(own_part.shape, jnp.bfloat16),
        in_specs=[vmem] * 2,
        out_specs=vmem,
        compiler_params=pltpu.CompilerParams(vmem_limit_bytes=SMALL_VMEM),
        name="chip_sum",
    )(own_part, partner_part)


def exchanged(value, axis, flip):
    size = lax.axis_size(axis)
    return lax.ppermute(value, axis, [(d, d ^ flip) for d in range(size)])


def every_row(tokens, norm_gain, routes, gate_probs, w_gate_up, w_down):
    device_count = lax.axis_size(AXES)
    shard_count = lax.axis_size("fsdp")
    group_count = lax.axis_size("grp")
    same_core = [[d for d in range(device_count) if d % 2 == k] for k in range(2)]

    payload = row_payload(tokens, norm_gain, routes, gate_probs)
    column = [payload] + [exchanged(payload, "fsdp", k) for k in range(2, shard_count, 2)]
    column = stacked(column)
    plane = [exchanged(column, "grp", k) for k in range(1, group_count)]
    own = [column] + plane
    other = [exchanged(block, "fsdp", 1) for block in own]
    own_part, other_part = weighted_parts(own, other, [w_gate_up[0]], w_down, routes.shape[1])
    from_partner = exchanged(other_part, "fsdp", 1)
    summed = chip_sum(own_part, from_partner)
    returned = lax.all_to_all(summed, AXES, 0, 0, axis_index_groups=same_core, tiled=True)
    return jnp.sum(returned.astype(jnp.float32), axis=0).astype(jnp.bfloat16)


def routed_rows(tokens, norm_gain, routes, gate_probs, w_gate_up, w_down):
    group_count = lax.axis_size("grp")
    shard_count = lax.axis_size("fsdp")
    shard_index = lax.axis_index("fsdp")
    split_count = FF // w_down.shape[1]
    rows_dev, width = tokens.shape
    block_rows = rows_dev * shard_count
    capacity = slot_capacity(tokens, routes, w_down)
    normed = rms_normed(tokens, norm_gain)
    rows_all = lax.all_gather(normed, "fsdp", axis=0, tiled=True)
    probs_all = lax.all_gather(gate_probs, "fsdp", axis=0, tiled=True)
    routes_all = lax.all_gather(routes, "fsdp", axis=0, tiled=True)
    probs = probs_all.astype(jnp.float32)
    combine = probs / jnp.sum(probs, axis=-1, keepdims=True)
    targets = (
        jnp.arange(group_count, dtype=jnp.int32) * (shard_count // split_count)
        + shard_index // split_count
    )
    matched = routes_all[None, :, :] == targets[:, None, None]
    is_routed = jnp.any(matched, axis=-1)
    row_weight = jnp.sum(jnp.where(matched, combine[None, :, :], 0.0), axis=-1)
    row_ids = jnp.arange(block_rows, dtype=jnp.int32)
    earlier = row_ids[:, None] >= row_ids[None, :]
    slot_index = jnp.sum(is_routed[:, None, :] & earlier[None], axis=-1, dtype=jnp.int32) - 1
    select = (
        slot_index[:, None, :] == jnp.arange(capacity, dtype=jnp.int32)[None, :, None]
    ) & is_routed[:, None, :]
    outgoing = jnp.einsum(
        "gcb,bd->gcd", select.astype(jnp.bfloat16), rows_all, preferred_element_type=jnp.float32
    ).astype(jnp.bfloat16)
    incoming = lax.all_to_all(outgoing, "grp", split_axis=0, concat_axis=0, tiled=True)
    result = expert_mlp(incoming.reshape(-1, width), w_gate_up, w_down)
    returned = lax.all_to_all(
        result.reshape(incoming.shape), "grp", split_axis=0, concat_axis=0, tiled=True
    )
    mix_matrix = (select.astype(jnp.float32) * row_weight[:, None, :]).reshape(-1, block_rows)
    row_partial = jnp.dot(
        mix_matrix.T,
        returned.reshape(-1, width),
        precision=lax.Precision.HIGHEST,
        preferred_element_type=jnp.float32,
    )
    summed = lax.psum_scatter(row_partial, "fsdp", scatter_dimension=0, tiled=True)
    return summed.astype(jnp.bfloat16)


def slot_capacity(tokens, routes, w_down):
    block_rows = tokens.shape[0] * lax.axis_size("fsdp")
    expert_count = lax.axis_size(AXES) * w_down.shape[1] // FF
    return 2 * block_rows * routes.shape[1] // expert_count


def local(tokens, norm_gain, routes, gate_probs, w_gate_up, w_down):
    block_rows = tokens.shape[0] * lax.axis_size("fsdp")
    dense = block_rows <= 2 * slot_capacity(tokens, routes, w_down)
    paired = lax.axis_size("fsdp") > 1 and lax.axis_size(AXES) & (lax.axis_size(AXES) - 1) == 0
    plan = every_row if dense and paired else routed_rows
    return plan(tokens, norm_gain, routes, gate_probs, w_gate_up, w_down)


def solution(mesh):
    return jax.shard_map(
        local,
        mesh=mesh,
        in_specs=(
            P(AXES, None),
            P(),
            P(AXES, None),
            P(AXES, None),
            P(AXES, None, None),
            P(AXES, None, None),
        ),
        out_specs=P(AXES, None),
        check_vma=False,
    )
```

```python
import math

import jax
import jax.numpy as jnp
from jax import lax
from jax.experimental import pallas as pl
from jax.experimental.pallas import tpu as pltpu
from jax.sharding import PartitionSpec as P

FF = 1024
LANES = 128
SMALL_VMEM = 2 << 20
MLP_VMEM = 24 << 20
MLP_TILE = 512
PREFETCH_WINDOW = pl.CostEstimate(flops=64 << 30, transcendentals=0, bytes_accessed=256 << 20)
AXES = ("grp", "fsdp")


def device_index():
    return lax.axis_index("grp") * lax.axis_size("fsdp") + lax.axis_index("fsdp")


def rms_normed(tokens, norm_gain):
    as_float = tokens.astype(jnp.float32)
    mean_square = jnp.mean(as_float * as_float, axis=-1, keepdims=True)
    return (as_float * lax.rsqrt(mean_square + 1e-06) * norm_gain).astype(jnp.bfloat16)


def expert_mlp(rows, w_gate_up, w_down):
    hidden_dev = w_down.shape[1]
    projected = jnp.dot(rows, w_gate_up[0], preferred_element_type=jnp.float32)
    hidden = (jax.nn.silu(projected[:, :hidden_dev]) * projected[:, hidden_dev:]).astype(
        jnp.bfloat16
    )
    return jnp.dot(hidden, w_down[0], preferred_element_type=jnp.float32).astype(jnp.bfloat16)


def row_payload(tokens, norm_gain, routes, gate_probs):
    rows_dev, width = tokens.shape
    top_count = routes.shape[1]
    total = width + LANES * -(-2 * top_count // LANES)

    def kernel(*refs):
        sources, payload_ref, targets, sems = refs[:4], refs[4], refs[5:9], refs[9]
        copies = [
            pltpu.make_async_copy(source, target, sems.at[index])
            for index, (source, target) in enumerate(zip(sources, targets))
        ]
        for copy in copies:
            copy.start()
        for copy in copies:
            copy.wait()
        tokens_ref, gain_ref, routes_ref, probs_ref = targets
        as_float = tokens_ref[...].astype(jnp.float32)
        mean_square = jnp.mean(as_float * as_float, axis=-1, keepdims=True)
        scaled = as_float * lax.rsqrt(mean_square + 1e-06) * gain_ref[...]
        payload_ref[:, :width] = scaled.astype(jnp.bfloat16)
        control = jnp.concatenate(
            [
                routes_ref[...].astype(jnp.float32),
                probs_ref[...].astype(jnp.float32),
                jnp.zeros((rows_dev, total - width - 2 * top_count), jnp.float32),
            ],
            axis=1,
        )
        payload_ref[:, width:] = control.astype(jnp.bfloat16)

    operands = (tokens, norm_gain.reshape(1, width), routes, gate_probs)
    return pl.pallas_call(
        kernel,
        out_shape=jax.ShapeDtypeStruct((rows_dev, total), jnp.bfloat16),
        in_specs=[pl.BlockSpec(memory_space=pltpu.HBM)] * 4,
        out_specs=pl.BlockSpec(memory_space=pltpu.VMEM),
        scratch_shapes=[pltpu.VMEM(o.shape, o.dtype) for o in operands]
        + [pltpu.SemaphoreType.DMA((4,))],
        compiler_params=pltpu.CompilerParams(vmem_limit_bytes=SMALL_VMEM),
        name="row_payload",
    )(*[pltpu.with_memory_space_constraint(o, pltpu.HBM) for o in operands])


def stacked(pieces):
    def kernel(*refs):
        for index, ref in enumerate(refs[:-1]):
            refs[-1][index] = ref[...]

    vmem = pl.BlockSpec(memory_space=pltpu.VMEM)
    return pl.pallas_call(
        kernel,
        out_shape=jax.ShapeDtypeStruct((len(pieces),) + pieces[0].shape, pieces[0].dtype),
        in_specs=[vmem] * len(pieces),
        out_specs=vmem,
        compiler_params=pltpu.CompilerParams(vmem_limit_bytes=SMALL_VMEM),
        cost_estimate=PREFETCH_WINDOW,
        name="stacked",
    )(*pieces)


def weighted_parts(own, other, gate_up_pieces, w_down, top_count):
    hidden_dev, width = w_down.shape[1:]
    blocks = list(own) + list(other)
    block_rows = blocks[0].shape[0] * blocks[0].shape[1]
    total = blocks[0].shape[2]
    row_count = block_rows * len(blocks)
    half = width // 2
    piece_count = len(gate_up_pieces)
    tile = math.gcd(math.gcd(hidden_dev, half), MLP_TILE)
    out_block = (row_count // blocks[0].shape[1], blocks[0].shape[1], half)

    def projected(rows_ref, piece_refs, column):
        sum_so_far, first = None, 0
        for piece in piece_refs:
            last = first + piece.shape[0]
            term = jnp.dot(
                rows_ref[:, first:last],
                piece[:, pl.ds(column, tile)],
                preferred_element_type=jnp.float32,
            )
            sum_so_far, first = term if sum_so_far is None else sum_so_far + term, last
        return sum_so_far

    def kernel(*refs):
        my_expert = device_index() // (FF // hidden_dev)
        block_refs, refs = refs[: len(blocks)], refs[len(blocks) :]
        piece_refs, refs = refs[:piece_count], refs[piece_count:]
        down_hbm, own_out, other_out, rows_ref, hidden_ref, down_ref, sem = refs
        fetch = pltpu.make_async_copy(down_hbm.at[0], down_ref, sem)
        fetch.start()
        for index, source in enumerate(block_refs):
            rows_ref[index * block_rows : (index + 1) * block_rows, :] = source[...].reshape(
                block_rows, total
            )
        control = rows_ref[:, width:].astype(jnp.float32)
        sent_routes = control[:, :top_count].astype(jnp.int32)
        probs = control[:, top_count : 2 * top_count]
        combine = probs / jnp.sum(probs, axis=-1, keepdims=True)
        row_weight = jnp.sum(
            jnp.where(sent_routes == my_expert, combine, 0.0), axis=-1, keepdims=True
        )
        @pl.loop(0, hidden_dev // tile)
        def _(step):
            column = pl.multiple_of(step * tile, tile)
            gate = projected(rows_ref, piece_refs, column)
            up = projected(rows_ref, piece_refs, pl.multiple_of(hidden_dev + column, tile))
            hidden_ref[:, pl.ds(column, tile)] = (jax.nn.silu(gate) * up).astype(jnp.bfloat16)

        fetch.wait()
        core = lax.rem(lax.axis_index("fsdp"), 2)
        for out, first in ((own_out, core * half), (other_out, (1 - core) * half)):
            for column in range(0, half, tile):
                part = jnp.dot(
                    hidden_ref[...],
                    down_ref[:, pl.ds(pl.multiple_of(first + column, tile), tile)],
                    preferred_element_type=jnp.float32,
                )
                weighted = part.astype(jnp.bfloat16).astype(jnp.float32) * row_weight
                out[:, :, column : column + tile] = weighted.reshape(
                    out_block[:2] + (tile,)
                ).astype(out.dtype)

    vmem = pl.BlockSpec(memory_space=pltpu.VMEM)
    return pl.pallas_call(
        kernel,
        out_shape=[
            jax.ShapeDtypeStruct(out_block, jnp.float32),
            jax.ShapeDtypeStruct(out_block, jnp.bfloat16),
        ],
        in_specs=[vmem] * (len(blocks) + piece_count)
        + [pl.BlockSpec(memory_space=pltpu.HBM)],
        out_specs=[vmem] * 2,
        scratch_shapes=[
            pltpu.VMEM((row_count, total), jnp.bfloat16),
            pltpu.VMEM((row_count, hidden_dev), jnp.bfloat16),
            pltpu.VMEM(w_down.shape[1:], w_down.dtype),
            pltpu.SemaphoreType.DMA,
        ],
        compiler_params=pltpu.CompilerParams(vmem_limit_bytes=MLP_VMEM),
        name="weighted_parts",
    )(
        *blocks,
        *[pltpu.with_memory_space_constraint(piece, pltpu.VMEM) for piece in gate_up_pieces],
        pltpu.with_memory_space_constraint(w_down, pltpu.HBM),
    )


def chip_sum(own_part, partner_part):
    pair_count = own_part.shape[0] // 2

    def kernel(own_ref, partner_ref, sum_ref):
        me = device_index()
        core = lax.rem(me, 2)
        for chip in range(pair_count):
            same = jnp.bitwise_xor(me // 2, chip)
            flip = pair_count + same
            for mine, theirs, place in ((same, flip, core), (flip, same, 1 - core)):
                total = own_ref[mine] + partner_ref[theirs].astype(jnp.float32)
                sum_ref[2 * chip + place] = total.astype(jnp.bfloat16)

    vmem = pl.BlockSpec(memory_space=pltpu.VMEM)
    return pl.pallas_call(
        kernel,
        out_shape=jax.ShapeDtypeStruct(own_part.shape, jnp.bfloat16),
        in_specs=[vmem] * 2,
        out_specs=vmem,
        compiler_params=pltpu.CompilerParams(vmem_limit_bytes=SMALL_VMEM),
        name="chip_sum",
    )(own_part, partner_part)


def row_sum(returned):
    device_count, rows_dev, half = returned.shape

    def kernel(returned_ref, out_ref):
        for core in range(2):
            total = returned_ref[core].astype(jnp.float32)
            for device in range(core + 2, device_count, 2):
                total += returned_ref[device].astype(jnp.float32)
            out_ref[:, core * half : (core + 1) * half] = total.astype(jnp.bfloat16)

    vmem = pl.BlockSpec(memory_space=pltpu.VMEM)
    return pl.pallas_call(
        kernel,
        out_shape=jax.ShapeDtypeStruct((rows_dev, 2 * half), jnp.bfloat16),
        in_specs=[vmem],
        out_specs=vmem,
        compiler_params=pltpu.CompilerParams(vmem_limit_bytes=SMALL_VMEM),
        name="row_sum",
    )(returned)


def exchanged(value, axis, flip):
    size = lax.axis_size(axis)
    return lax.ppermute(value, axis, [(d, d ^ flip) for d in range(size)])


def every_row(tokens, norm_gain, routes, gate_probs, w_gate_up, w_down):
    shard_count = lax.axis_size("fsdp")
    group_count = lax.axis_size("grp")

    payload = row_payload(tokens, norm_gain, routes, gate_probs)
    column = [payload] + [exchanged(payload, "fsdp", k) for k in range(2, shard_count, 2)]
    column = stacked(column)
    plane = [exchanged(column, "grp", k) for k in range(1, group_count)]
    own = [column] + plane
    other = [exchanged(block, "fsdp", 1) for block in own]
    own_part, other_part = weighted_parts(own, other, [w_gate_up[0]], w_down, routes.shape[1])
    from_partner = exchanged(other_part, "fsdp", 1)
    summed = chip_sum(own_part, from_partner)
    return row_sum(lax.all_to_all(summed, AXES, 0, 0, tiled=True))


def routed_rows(tokens, norm_gain, routes, gate_probs, w_gate_up, w_down):
    group_count = lax.axis_size("grp")
    shard_count = lax.axis_size("fsdp")
    shard_index = lax.axis_index("fsdp")
    split_count = FF // w_down.shape[1]
    rows_dev, width = tokens.shape
    block_rows = rows_dev * shard_count
    capacity = slot_capacity(tokens, routes, w_down)
    normed = rms_normed(tokens, norm_gain)
    rows_all = lax.all_gather(normed, "fsdp", axis=0, tiled=True)
    probs_all = lax.all_gather(gate_probs, "fsdp", axis=0, tiled=True)
    routes_all = lax.all_gather(routes, "fsdp", axis=0, tiled=True)
    probs = probs_all.astype(jnp.float32)
    combine = probs / jnp.sum(probs, axis=-1, keepdims=True)
    targets = (
        jnp.arange(group_count, dtype=jnp.int32) * (shard_count // split_count)
        + shard_index // split_count
    )
    matched = routes_all[None, :, :] == targets[:, None, None]
    is_routed = jnp.any(matched, axis=-1)
    row_weight = jnp.sum(jnp.where(matched, combine[None, :, :], 0.0), axis=-1)
    row_ids = jnp.arange(block_rows, dtype=jnp.int32)
    earlier = row_ids[:, None] >= row_ids[None, :]
    slot_index = jnp.sum(is_routed[:, None, :] & earlier[None], axis=-1, dtype=jnp.int32) - 1
    select = (
        slot_index[:, None, :] == jnp.arange(capacity, dtype=jnp.int32)[None, :, None]
    ) & is_routed[:, None, :]
    outgoing = jnp.einsum(
        "gcb,bd->gcd", select.astype(jnp.bfloat16), rows_all, preferred_element_type=jnp.float32
    ).astype(jnp.bfloat16)
    incoming = lax.all_to_all(outgoing, "grp", split_axis=0, concat_axis=0, tiled=True)
    result = expert_mlp(incoming.reshape(-1, width), w_gate_up, w_down)
    returned = lax.all_to_all(
        result.reshape(incoming.shape), "grp", split_axis=0, concat_axis=0, tiled=True
    )
    mix_matrix = (select.astype(jnp.float32) * row_weight[:, None, :]).reshape(-1, block_rows)
    row_partial = jnp.dot(
        mix_matrix.T,
        returned.reshape(-1, width),
        precision=lax.Precision.HIGHEST,
        preferred_element_type=jnp.float32,
    )
    summed = lax.psum_scatter(row_partial, "fsdp", scatter_dimension=0, tiled=True)
    return summed.astype(jnp.bfloat16)


def slot_capacity(tokens, routes, w_down):
    block_rows = tokens.shape[0] * lax.axis_size("fsdp")
    expert_count = lax.axis_size(AXES) * w_down.shape[1] // FF
    return 2 * block_rows * routes.shape[1] // expert_count


def local(tokens, norm_gain, routes, gate_probs, w_gate_up, w_down):
    block_rows = tokens.shape[0] * lax.axis_size("fsdp")
    dense = block_rows <= 2 * slot_capacity(tokens, routes, w_down)
    paired = lax.axis_size("fsdp") > 1 and lax.axis_size(AXES) & (lax.axis_size(AXES) - 1) == 0
    plan = every_row if dense and paired else routed_rows
    return plan(tokens, norm_gain, routes, gate_probs, w_gate_up, w_down)


def solution(mesh):
    return jax.shard_map(
        local,
        mesh=mesh,
        in_specs=(
            P(AXES, None),
            P(),
            P(AXES, None),
            P(AXES, None),
            P(AXES, None, None),
            P(AXES, None, None),
        ),
        out_specs=P(AXES, None),
        check_vma=False,
    )
```

```python
import math

import jax
import jax.numpy as jnp
from jax import lax
from jax.experimental import pallas as pl
from jax.experimental.pallas import tpu as pltpu
from jax.sharding import PartitionSpec as P

FF = 1024
LANES = 128
SMALL_VMEM = 2 << 20
MLP_VMEM = 24 << 20
MLP_TILE = 512
PREFETCH_WINDOW = pl.CostEstimate(flops=64 << 30, transcendentals=0, bytes_accessed=256 << 20)
AXES = ("grp", "fsdp")


def device_index():
    return lax.axis_index("grp") * lax.axis_size("fsdp") + lax.axis_index("fsdp")


def rms_normed(tokens, norm_gain):
    as_float = tokens.astype(jnp.float32)
    mean_square = jnp.mean(as_float * as_float, axis=-1, keepdims=True)
    return (as_float * lax.rsqrt(mean_square + 1e-06) * norm_gain).astype(jnp.bfloat16)


def expert_mlp(rows, w_gate_up, w_down):
    hidden_dev = w_down.shape[1]
    projected = jnp.dot(rows, w_gate_up[0], preferred_element_type=jnp.float32)
    hidden = (jax.nn.silu(projected[:, :hidden_dev]) * projected[:, hidden_dev:]).astype(
        jnp.bfloat16
    )
    return jnp.dot(hidden, w_down[0], preferred_element_type=jnp.float32).astype(jnp.bfloat16)


def row_payload(tokens, norm_gain, routes, gate_probs):
    rows_dev, width = tokens.shape
    top_count = routes.shape[1]
    total = width + LANES * -(-2 * top_count // LANES)

    def kernel(*refs):
        sources, payload_ref, targets, sems = refs[:4], refs[4], refs[5:9], refs[9]
        copies = [
            pltpu.make_async_copy(source, target, sems.at[index])
            for index, (source, target) in enumerate(zip(sources, targets))
        ]
        for copy in copies:
            copy.start()
        for copy in copies:
            copy.wait()
        tokens_ref, gain_ref, routes_ref, probs_ref = targets
        as_float = tokens_ref[...].astype(jnp.float32)
        mean_square = jnp.mean(as_float * as_float, axis=-1, keepdims=True)
        scaled = as_float * lax.rsqrt(mean_square + 1e-06) * gain_ref[...]
        payload_ref[:, :width] = scaled.astype(jnp.bfloat16)
        control = jnp.concatenate(
            [
                routes_ref[...].astype(jnp.float32),
                probs_ref[...].astype(jnp.float32),
                jnp.zeros((rows_dev, total - width - 2 * top_count), jnp.float32),
            ],
            axis=1,
        )
        payload_ref[:, width:] = control.astype(jnp.bfloat16)

    operands = (tokens, norm_gain.reshape(1, width), routes, gate_probs)
    return pl.pallas_call(
        kernel,
        out_shape=jax.ShapeDtypeStruct((rows_dev, total), jnp.bfloat16),
        in_specs=[pl.BlockSpec(memory_space=pltpu.HBM)] * 4,
        out_specs=pl.BlockSpec(memory_space=pltpu.VMEM),
        scratch_shapes=[pltpu.VMEM(o.shape, o.dtype) for o in operands]
        + [pltpu.SemaphoreType.DMA((4,))],
        compiler_params=pltpu.CompilerParams(vmem_limit_bytes=SMALL_VMEM),
        name="row_payload",
    )(*[pltpu.with_memory_space_constraint(o, pltpu.HBM) for o in operands])


def stacked(pieces):
    def kernel(*refs):
        for index, ref in enumerate(refs[:-1]):
            refs[-1][index] = ref[...]

    vmem = pl.BlockSpec(memory_space=pltpu.VMEM)
    return pl.pallas_call(
        kernel,
        out_shape=jax.ShapeDtypeStruct((len(pieces),) + pieces[0].shape, pieces[0].dtype),
        in_specs=[vmem] * len(pieces),
        out_specs=vmem,
        compiler_params=pltpu.CompilerParams(vmem_limit_bytes=SMALL_VMEM),
        cost_estimate=PREFETCH_WINDOW,
        name="stacked",
    )(*pieces)


def weighted_parts(own, other, gate_up_pieces, w_down, top_count):
    hidden_dev, width = w_down.shape[1:]
    blocks = list(own) + list(other)
    block_rows = blocks[0].shape[0] * blocks[0].shape[1]
    total = blocks[0].shape[2]
    row_count = block_rows * len(blocks)
    half = width // 2
    piece_count = len(gate_up_pieces)
    tile = math.gcd(math.gcd(hidden_dev, half), MLP_TILE)
    out_block = (row_count // blocks[0].shape[1], blocks[0].shape[1], half)

    def projected(rows_ref, piece_refs, column):
        sum_so_far, first = None, 0
        for piece in piece_refs:
            last = first + piece.shape[0]
            term = jnp.dot(
                rows_ref[:, first:last],
                piece[:, pl.ds(column, tile)],
                preferred_element_type=jnp.float32,
            )
            sum_so_far, first = term if sum_so_far is None else sum_so_far + term, last
        return sum_so_far

    def kernel(*refs):
        my_expert = device_index() // (FF // hidden_dev)
        block_refs, refs = refs[: len(blocks)], refs[len(blocks) :]
        piece_refs, refs = refs[:piece_count], refs[piece_count:]
        down_hbm, other_out, hidden_ref, weight_out, down_own, rows_ref, down_ref, sems = refs
        core = lax.rem(lax.axis_index("fsdp"), 2)
        fetches = [
            pltpu.make_async_copy(
                down_hbm.at[0, :, pl.ds(pl.multiple_of(place * half, half), half)],
                target,
                sems.at[index],
            )
            for index, (place, target) in enumerate(((1 - core, down_ref), (core, down_own)))
        ]
        for fetch in fetches:
            fetch.start()
        for index, source in enumerate(block_refs):
            rows_ref[index * block_rows : (index + 1) * block_rows, :] = source[...].reshape(
                block_rows, total
            )
        control = rows_ref[:, width:].astype(jnp.float32)
        sent_routes = control[:, :top_count].astype(jnp.int32)
        probs = control[:, top_count : 2 * top_count]
        combine = probs / jnp.sum(probs, axis=-1, keepdims=True)
        row_weight = jnp.sum(
            jnp.where(sent_routes == my_expert, combine, 0.0), axis=-1, keepdims=True
        )
        @pl.loop(0, hidden_dev // tile)
        def _(step):
            column = pl.multiple_of(step * tile, tile)
            gate = projected(rows_ref, piece_refs, column)
            up = projected(rows_ref, piece_refs, pl.multiple_of(hidden_dev + column, tile))
            hidden_ref[:, pl.ds(column, tile)] = (jax.nn.silu(gate) * up).astype(jnp.bfloat16)

        for fetch in fetches:
            fetch.wait()
        weight_out[...] = jnp.broadcast_to(row_weight, weight_out.shape)
        weighted_columns(hidden_ref, down_ref, row_weight, other_out, tile)

    vmem = pl.BlockSpec(memory_space=pltpu.VMEM)
    return pl.pallas_call(
        kernel,
        out_shape=[
            jax.ShapeDtypeStruct(out_block, jnp.bfloat16),
            jax.ShapeDtypeStruct((row_count, hidden_dev), jnp.bfloat16),
            jax.ShapeDtypeStruct((row_count, LANES), jnp.float32),
            pltpu.VMEM((hidden_dev, half), w_down.dtype),
        ],
        in_specs=[vmem] * (len(blocks) + piece_count)
        + [pl.BlockSpec(memory_space=pltpu.HBM)],
        out_specs=[vmem] * 4,
        scratch_shapes=[
            pltpu.VMEM((row_count, total), jnp.bfloat16),
            pltpu.VMEM((hidden_dev, half), w_down.dtype),
            pltpu.SemaphoreType.DMA((2,)),
        ],
        compiler_params=pltpu.CompilerParams(vmem_limit_bytes=MLP_VMEM),
        name="weighted_parts",
    )(
        *blocks,
        *[pltpu.with_memory_space_constraint(piece, pltpu.VMEM) for piece in gate_up_pieces],
        pltpu.with_memory_space_constraint(w_down, pltpu.HBM),
    )


def weighted_columns(hidden_ref, down_ref, row_weight, out, tile):
    for column in range(0, down_ref.shape[1], tile):
        columns = slice(column, column + tile)
        part = jnp.dot(hidden_ref[...], down_ref[:, columns], preferred_element_type=jnp.float32)
        weighted = part.astype(jnp.bfloat16).astype(jnp.float32) * row_weight
        out[:, :, columns] = weighted.reshape(out.shape[:2] + (tile,)).astype(out.dtype)


def own_columns(hidden, weight, down_own, out_block):
    tile = math.gcd(out_block[2], MLP_TILE)

    def kernel(hidden_ref, weight_ref, down_ref, out):
        weighted_columns(hidden_ref, down_ref, weight_ref[:, :1], out, tile)

    vmem = pl.BlockSpec(memory_space=pltpu.VMEM)
    return pl.pallas_call(
        kernel,
        out_shape=jax.ShapeDtypeStruct(out_block, jnp.float32),
        in_specs=[vmem] * 3,
        out_specs=vmem,
        compiler_params=pltpu.CompilerParams(vmem_limit_bytes=MLP_VMEM),
        cost_estimate=pl.CostEstimate(
            flops=2 * hidden.shape[0] * down_own.size, transcendentals=0, bytes_accessed=down_own.nbytes
        ),
        name="own_columns",
    )(hidden, weight, pltpu.with_memory_space_constraint(down_own, pltpu.VMEM))


def chip_sum(own_part, partner_part):
    pair_count = own_part.shape[0] // 2

    def kernel(own_ref, partner_ref, sum_ref):
        me = device_index()
        core = lax.rem(me, 2)
        for chip in range(pair_count):
            same = jnp.bitwise_xor(me // 2, chip)
            flip = pair_count + same
            for mine, theirs, place in ((same, flip, core), (flip, same, 1 - core)):
                total = own_ref[mine] + partner_ref[theirs].astype(jnp.float32)
                sum_ref[2 * chip + place] = total.astype(jnp.bfloat16)

    vmem = pl.BlockSpec(memory_space=pltpu.VMEM)
    return pl.pallas_call(
        kernel,
        out_shape=jax.ShapeDtypeStruct(own_part.shape, jnp.bfloat16),
        in_specs=[vmem] * 2,
        out_specs=vmem,
        compiler_params=pltpu.CompilerParams(vmem_limit_bytes=SMALL_VMEM),
        name="chip_sum",
    )(own_part, partner_part)


def row_sum(returned):
    device_count, rows_dev, half = returned.shape

    def kernel(returned_ref, out_ref):
        for core in range(2):
            total = returned_ref[core].astype(jnp.float32)
            for device in range(core + 2, device_count, 2):
                total += returned_ref[device].astype(jnp.float32)
            out_ref[:, core * half : (core + 1) * half] = total.astype(jnp.bfloat16)

    vmem = pl.BlockSpec(memory_space=pltpu.VMEM)
    return pl.pallas_call(
        kernel,
        out_shape=jax.ShapeDtypeStruct((rows_dev, 2 * half), jnp.bfloat16),
        in_specs=[vmem],
        out_specs=vmem,
        compiler_params=pltpu.CompilerParams(vmem_limit_bytes=SMALL_VMEM),
        name="row_sum",
    )(returned)


def exchanged(value, axis, flip):
    size = lax.axis_size(axis)
    return lax.ppermute(value, axis, [(d, d ^ flip) for d in range(size)])


def every_row(tokens, norm_gain, routes, gate_probs, w_gate_up, w_down):
    shard_count = lax.axis_size("fsdp")
    group_count = lax.axis_size("grp")

    payload = row_payload(tokens, norm_gain, routes, gate_probs)
    column = [payload] + [exchanged(payload, "fsdp", k) for k in range(2, shard_count, 2)]
    column = stacked(column)
    plane = [exchanged(column, "grp", k) for k in range(1, group_count)]
    own = [column] + plane
    other = [exchanged(block, "fsdp", 1) for block in own]
    other_part, hidden, weight, down_own = weighted_parts(own, other, [w_gate_up[0]], w_down, routes.shape[1])
    from_partner = exchanged(other_part, "fsdp", 1)
    own_part = own_columns(hidden, weight, down_own, other_part.shape)
    summed = chip_sum(own_part, from_partner)
    return row_sum(lax.all_to_all(summed, AXES, 0, 0, tiled=True))


def routed_rows(tokens, norm_gain, routes, gate_probs, w_gate_up, w_down):
    group_count = lax.axis_size("grp")
    shard_count = lax.axis_size("fsdp")
    shard_index = lax.axis_index("fsdp")
    split_count = FF // w_down.shape[1]
    rows_dev, width = tokens.shape
    block_rows = rows_dev * shard_count
    capacity = slot_capacity(tokens, routes, w_down)
    normed = rms_normed(tokens, norm_gain)
    rows_all = lax.all_gather(normed, "fsdp", axis=0, tiled=True)
    probs_all = lax.all_gather(gate_probs, "fsdp", axis=0, tiled=True)
    routes_all = lax.all_gather(routes, "fsdp", axis=0, tiled=True)
    probs = probs_all.astype(jnp.float32)
    combine = probs / jnp.sum(probs, axis=-1, keepdims=True)
    targets = (
        jnp.arange(group_count, dtype=jnp.int32) * (shard_count // split_count)
        + shard_index // split_count
    )
    matched = routes_all[None, :, :] == targets[:, None, None]
    is_routed = jnp.any(matched, axis=-1)
    row_weight = jnp.sum(jnp.where(matched, combine[None, :, :], 0.0), axis=-1)
    row_ids = jnp.arange(block_rows, dtype=jnp.int32)
    earlier = row_ids[:, None] >= row_ids[None, :]
    slot_index = jnp.sum(is_routed[:, None, :] & earlier[None], axis=-1, dtype=jnp.int32) - 1
    select = (
        slot_index[:, None, :] == jnp.arange(capacity, dtype=jnp.int32)[None, :, None]
    ) & is_routed[:, None, :]
    outgoing = jnp.einsum(
        "gcb,bd->gcd", select.astype(jnp.bfloat16), rows_all, preferred_element_type=jnp.float32
    ).astype(jnp.bfloat16)
    incoming = lax.all_to_all(outgoing, "grp", split_axis=0, concat_axis=0, tiled=True)
    result = expert_mlp(incoming.reshape(-1, width), w_gate_up, w_down)
    returned = lax.all_to_all(
        result.reshape(incoming.shape), "grp", split_axis=0, concat_axis=0, tiled=True
    )
    mix_matrix = (select.astype(jnp.float32) * row_weight[:, None, :]).reshape(-1, block_rows)
    row_partial = jnp.dot(
        mix_matrix.T,
        returned.reshape(-1, width),
        precision=lax.Precision.HIGHEST,
        preferred_element_type=jnp.float32,
    )
    summed = lax.psum_scatter(row_partial, "fsdp", scatter_dimension=0, tiled=True)
    return summed.astype(jnp.bfloat16)


def slot_capacity(tokens, routes, w_down):
    block_rows = tokens.shape[0] * lax.axis_size("fsdp")
    expert_count = lax.axis_size(AXES) * w_down.shape[1] // FF
    return 2 * block_rows * routes.shape[1] // expert_count


def local(tokens, norm_gain, routes, gate_probs, w_gate_up, w_down):
    block_rows = tokens.shape[0] * lax.axis_size("fsdp")
    dense = block_rows <= 2 * slot_capacity(tokens, routes, w_down)
    paired = lax.axis_size("fsdp") > 1 and lax.axis_size(AXES) & (lax.axis_size(AXES) - 1) == 0
    plan = every_row if dense and paired else routed_rows
    return plan(tokens, norm_gain, routes, gate_probs, w_gate_up, w_down)


def solution(mesh):
    return jax.shard_map(
        local,
        mesh=mesh,
        in_specs=(
            P(AXES, None),
            P(),
            P(AXES, None),
            P(AXES, None),
            P(AXES, None, None),
            P(AXES, None, None),
        ),
        out_specs=P(AXES, None),
        check_vma=False,
    )
```

```python
import math

import jax
import jax.numpy as jnp
from jax import lax
from jax.experimental import pallas as pl
from jax.experimental.pallas import tpu as pltpu
from jax.sharding import PartitionSpec as P

FF = 1024
LANES = 128
SMALL_VMEM = 2 << 20
MLP_VMEM = 8 << 20
MLP_TILE = 512
PREFETCH_WINDOW = pl.CostEstimate(flops=64 << 30, transcendentals=0, bytes_accessed=256 << 20)
AXES = ("grp", "fsdp")


def device_index():
    return lax.axis_index("grp") * lax.axis_size("fsdp") + lax.axis_index("fsdp")


def rms_normed(tokens, norm_gain):
    as_float = tokens.astype(jnp.float32)
    mean_square = jnp.mean(as_float * as_float, axis=-1, keepdims=True)
    return (as_float * lax.rsqrt(mean_square + 1e-06) * norm_gain).astype(jnp.bfloat16)


def expert_mlp(rows, w_gate_up, w_down):
    hidden_dev = w_down.shape[1]
    projected = jnp.dot(rows, w_gate_up[0], preferred_element_type=jnp.float32)
    hidden = (jax.nn.silu(projected[:, :hidden_dev]) * projected[:, hidden_dev:]).astype(
        jnp.bfloat16
    )
    return jnp.dot(hidden, w_down[0], preferred_element_type=jnp.float32).astype(jnp.bfloat16)


def row_payload(tokens, norm_gain, routes, gate_probs):
    rows_dev, width = tokens.shape
    top_count = routes.shape[1]
    total = width + LANES * -(-2 * top_count // LANES)

    def kernel(*refs):
        sources, payload_ref, targets, sems = refs[:4], refs[4], refs[5:9], refs[9]
        copies = [
            pltpu.make_async_copy(source, target, sems.at[index])
            for index, (source, target) in enumerate(zip(sources, targets))
        ]
        for copy in copies:
            copy.start()
        for copy in copies:
            copy.wait()
        tokens_ref, gain_ref, routes_ref, probs_ref = targets
        as_float = tokens_ref[...].astype(jnp.float32)
        mean_square = jnp.mean(as_float * as_float, axis=-1, keepdims=True)
        scaled = as_float * lax.rsqrt(mean_square + 1e-06) * gain_ref[...]
        payload_ref[:, :width] = scaled.astype(jnp.bfloat16)
        control = jnp.concatenate(
            [
                routes_ref[...].astype(jnp.float32),
                probs_ref[...].astype(jnp.float32),
                jnp.zeros((rows_dev, total - width - 2 * top_count), jnp.float32),
            ],
            axis=1,
        )
        payload_ref[:, width:] = control.astype(jnp.bfloat16)

    operands = (tokens, norm_gain.reshape(1, width), routes, gate_probs)
    return pl.pallas_call(
        kernel,
        out_shape=jax.ShapeDtypeStruct((rows_dev, total), jnp.bfloat16),
        in_specs=[pl.BlockSpec(memory_space=pltpu.HBM)] * 4,
        out_specs=pl.BlockSpec(memory_space=pltpu.VMEM),
        scratch_shapes=[pltpu.VMEM(o.shape, o.dtype) for o in operands]
        + [pltpu.SemaphoreType.DMA((4,))],
        compiler_params=pltpu.CompilerParams(vmem_limit_bytes=SMALL_VMEM),
        name="row_payload",
    )(*[pltpu.with_memory_space_constraint(o, pltpu.HBM) for o in operands])


def stacked(pieces):
    def kernel(*refs):
        for index, ref in enumerate(refs[:-1]):
            refs[-1][index] = ref[...]

    vmem = pl.BlockSpec(memory_space=pltpu.VMEM)
    return pl.pallas_call(
        kernel,
        out_shape=jax.ShapeDtypeStruct((len(pieces),) + pieces[0].shape, pieces[0].dtype),
        in_specs=[vmem] * len(pieces),
        out_specs=vmem,
        compiler_params=pltpu.CompilerParams(vmem_limit_bytes=SMALL_VMEM),
        cost_estimate=PREFETCH_WINDOW,
        name="stacked",
    )(*pieces)


def weighted_parts(own, other, gate_up_pieces, w_down, top_count):
    hidden_dev, width = w_down.shape
    blocks = list(own) + list(other)
    block_rows = blocks[0].shape[0] * blocks[0].shape[1]
    total = blocks[0].shape[2]
    row_count = block_rows * len(blocks)
    half = width // 2
    piece_count = len(gate_up_pieces)
    tile = math.gcd(math.gcd(hidden_dev, half), MLP_TILE)
    out_block = (row_count // blocks[0].shape[1], blocks[0].shape[1], half)

    def projected(rows_ref, piece_refs, column):
        sum_so_far, first = None, 0
        for piece in piece_refs:
            last = first + piece.shape[0]
            term = jnp.dot(
                rows_ref[:, first:last],
                piece[:, pl.ds(column, tile)],
                preferred_element_type=jnp.float32,
            )
            sum_so_far, first = term if sum_so_far is None else sum_so_far + term, last
        return sum_so_far

    def kernel(*refs):
        my_expert = device_index() // (FF // hidden_dev)
        block_refs, refs = refs[: len(blocks)], refs[len(blocks) :]
        piece_refs, refs = refs[:piece_count], refs[piece_count:]
        down_ref, other_out, hidden_ref, weight_out, rows_ref = refs
        core = lax.rem(lax.axis_index("fsdp"), 2)
        for index, source in enumerate(block_refs):
            rows_ref[index * block_rows : (index + 1) * block_rows, :] = source[...].reshape(
                block_rows, total
            )
        control = rows_ref[:, width:].astype(jnp.float32)
        sent_routes = control[:, :top_count].astype(jnp.int32)
        probs = control[:, top_count : 2 * top_count]
        combine = probs / jnp.sum(probs, axis=-1, keepdims=True)
        row_weight = jnp.sum(
            jnp.where(sent_routes == my_expert, combine, 0.0), axis=-1, keepdims=True
        )
        for column in range(0, hidden_dev, tile):
            gate = projected(rows_ref, piece_refs, column)
            up = projected(rows_ref, piece_refs, hidden_dev + column)
            hidden_ref[:, column : column + tile] = (jax.nn.silu(gate) * up).astype(jnp.bfloat16)
        weight_out[...] = jnp.broadcast_to(row_weight, weight_out.shape)
        weighted_columns(hidden_ref, down_ref, (1 - core) * half, row_weight, other_out, tile)

    vmem = pl.BlockSpec(memory_space=pltpu.VMEM)
    return pl.pallas_call(
        kernel,
        out_shape=[
            jax.ShapeDtypeStruct(out_block, jnp.bfloat16),
            jax.ShapeDtypeStruct((row_count, hidden_dev), jnp.bfloat16),
            jax.ShapeDtypeStruct((row_count, LANES), jnp.float32),
        ],
        in_specs=[vmem] * (len(blocks) + piece_count + 1),
        out_specs=[vmem] * 3,
        scratch_shapes=[
            pltpu.VMEM((row_count, total), jnp.bfloat16),
        ],
        compiler_params=pltpu.CompilerParams(vmem_limit_bytes=MLP_VMEM),
        name="weighted_parts",
    )(
        *blocks,
        *[pltpu.with_memory_space_constraint(piece, pltpu.VMEM) for piece in gate_up_pieces],
        pltpu.with_memory_space_constraint(w_down, pltpu.VMEM),
    )


def weighted_columns(hidden_ref, down_ref, first, row_weight, out, tile):
    for column in range(0, out.shape[2], tile):
        columns = slice(column, column + tile)
        source = pl.ds(pl.multiple_of(first + column, tile), tile)
        part = jnp.dot(hidden_ref[...], down_ref[:, source], preferred_element_type=jnp.float32)
        weighted = part.astype(jnp.bfloat16).astype(jnp.float32) * row_weight
        out[:, :, columns] = weighted.reshape(out.shape[:2] + (tile,)).astype(out.dtype)


def own_columns(hidden, weight, w_down, out_block):
    tile = math.gcd(out_block[2], MLP_TILE)

    def kernel(hidden_ref, weight_ref, down_ref, out):
        first = lax.rem(lax.axis_index("fsdp"), 2) * out_block[2]
        weighted_columns(hidden_ref, down_ref, first, weight_ref[:, :1], out, tile)

    vmem = pl.BlockSpec(memory_space=pltpu.VMEM)
    return pl.pallas_call(
        kernel,
        out_shape=jax.ShapeDtypeStruct(out_block, jnp.float32),
        in_specs=[vmem] * 3,
        out_specs=vmem,
        compiler_params=pltpu.CompilerParams(vmem_limit_bytes=MLP_VMEM),
        cost_estimate=pl.CostEstimate(
            flops=hidden.shape[0] * w_down.size, transcendentals=0, bytes_accessed=w_down.nbytes // 2
        ),
        name="own_columns",
    )(hidden, weight, pltpu.with_memory_space_constraint(w_down, pltpu.VMEM))


def chip_sum(own_part, partner_part):
    pair_count = own_part.shape[0] // 2

    def kernel(own_ref, partner_ref, sum_ref):
        me = device_index()
        core = lax.rem(me, 2)
        for chip in range(pair_count):
            same = jnp.bitwise_xor(me // 2, chip)
            flip = pair_count + same
            for mine, theirs, place in ((same, flip, core), (flip, same, 1 - core)):
                total = own_ref[mine] + partner_ref[theirs].astype(jnp.float32)
                sum_ref[2 * chip + place] = total.astype(jnp.bfloat16)

    vmem = pl.BlockSpec(memory_space=pltpu.VMEM)
    return pl.pallas_call(
        kernel,
        out_shape=jax.ShapeDtypeStruct(own_part.shape, jnp.bfloat16),
        in_specs=[vmem] * 2,
        out_specs=vmem,
        compiler_params=pltpu.CompilerParams(vmem_limit_bytes=SMALL_VMEM),
        name="chip_sum",
    )(own_part, partner_part)


def row_sum(returned):
    device_count, rows_dev, half = returned.shape

    def kernel(returned_ref, out_ref):
        for core in range(2):
            total = returned_ref[core].astype(jnp.float32)
            for device in range(core + 2, device_count, 2):
                total += returned_ref[device].astype(jnp.float32)
            out_ref[:, core * half : (core + 1) * half] = total.astype(jnp.bfloat16)

    vmem = pl.BlockSpec(memory_space=pltpu.VMEM)
    return pl.pallas_call(
        kernel,
        out_shape=jax.ShapeDtypeStruct((rows_dev, 2 * half), jnp.bfloat16),
        in_specs=[vmem],
        out_specs=vmem,
        compiler_params=pltpu.CompilerParams(vmem_limit_bytes=SMALL_VMEM),
        name="row_sum",
    )(returned)


def exchanged(value, axis, flip):
    size = lax.axis_size(axis)
    return lax.ppermute(value, axis, [(d, d ^ flip) for d in range(size)])


def every_row(tokens, norm_gain, routes, gate_probs, w_gate_up, w_down):
    shard_count = lax.axis_size("fsdp")
    group_count = lax.axis_size("grp")

    payload = row_payload(tokens, norm_gain, routes, gate_probs)
    column = [payload] + [exchanged(payload, "fsdp", k) for k in range(2, shard_count, 2)]
    column = stacked(column)
    plane = [exchanged(column, "grp", k) for k in range(1, group_count)]
    own = [column] + plane
    other = [exchanged(block, "fsdp", 1) for block in own]
    other_part, hidden, weight = weighted_parts(own, other, [w_gate_up[0]], w_down[0], routes.shape[1])
    from_partner = exchanged(other_part, "fsdp", 1)
    own_part = own_columns(hidden, weight, w_down[0], other_part.shape)
    summed = chip_sum(own_part, from_partner)
    return row_sum(lax.all_to_all(summed, AXES, 0, 0, tiled=True))


def routed_rows(tokens, norm_gain, routes, gate_probs, w_gate_up, w_down):
    group_count = lax.axis_size("grp")
    shard_count = lax.axis_size("fsdp")
    shard_index = lax.axis_index("fsdp")
    split_count = FF // w_down.shape[1]
    rows_dev, width = tokens.shape
    block_rows = rows_dev * shard_count
    capacity = slot_capacity(tokens, routes, w_down)
    normed = rms_normed(tokens, norm_gain)
    rows_all = lax.all_gather(normed, "fsdp", axis=0, tiled=True)
    probs_all = lax.all_gather(gate_probs, "fsdp", axis=0, tiled=True)
    routes_all = lax.all_gather(routes, "fsdp", axis=0, tiled=True)
    probs = probs_all.astype(jnp.float32)
    combine = probs / jnp.sum(probs, axis=-1, keepdims=True)
    targets = (
        jnp.arange(group_count, dtype=jnp.int32) * (shard_count // split_count)
        + shard_index // split_count
    )
    matched = routes_all[None, :, :] == targets[:, None, None]
    is_routed = jnp.any(matched, axis=-1)
    row_weight = jnp.sum(jnp.where(matched, combine[None, :, :], 0.0), axis=-1)
    row_ids = jnp.arange(block_rows, dtype=jnp.int32)
    earlier = row_ids[:, None] >= row_ids[None, :]
    slot_index = jnp.sum(is_routed[:, None, :] & earlier[None], axis=-1, dtype=jnp.int32) - 1
    select = (
        slot_index[:, None, :] == jnp.arange(capacity, dtype=jnp.int32)[None, :, None]
    ) & is_routed[:, None, :]
    outgoing = jnp.einsum(
        "gcb,bd->gcd", select.astype(jnp.bfloat16), rows_all, preferred_element_type=jnp.float32
    ).astype(jnp.bfloat16)
    incoming = lax.all_to_all(outgoing, "grp", split_axis=0, concat_axis=0, tiled=True)
    result = expert_mlp(incoming.reshape(-1, width), w_gate_up, w_down)
    returned = lax.all_to_all(
        result.reshape(incoming.shape), "grp", split_axis=0, concat_axis=0, tiled=True
    )
    mix_matrix = (select.astype(jnp.float32) * row_weight[:, None, :]).reshape(-1, block_rows)
    row_partial = jnp.dot(
        mix_matrix.T,
        returned.reshape(-1, width),
        precision=lax.Precision.HIGHEST,
        preferred_element_type=jnp.float32,
    )
    summed = lax.psum_scatter(row_partial, "fsdp", scatter_dimension=0, tiled=True)
    return summed.astype(jnp.bfloat16)


def slot_capacity(tokens, routes, w_down):
    block_rows = tokens.shape[0] * lax.axis_size("fsdp")
    expert_count = lax.axis_size(AXES) * w_down.shape[1] // FF
    return 2 * block_rows * routes.shape[1] // expert_count


def local(tokens, norm_gain, routes, gate_probs, w_gate_up, w_down):
    block_rows = tokens.shape[0] * lax.axis_size("fsdp")
    dense = block_rows <= 2 * slot_capacity(tokens, routes, w_down)
    paired = lax.axis_size("fsdp") > 1 and lax.axis_size(AXES) & (lax.axis_size(AXES) - 1) == 0
    plan = every_row if dense and paired else routed_rows
    return plan(tokens, norm_gain, routes, gate_probs, w_gate_up, w_down)


def solution(mesh):
    return jax.shard_map(
        local,
        mesh=mesh,
        in_specs=(
            P(AXES, None),
            P(),
            P(AXES, None),
            P(AXES, None),
            P(AXES, None, None),
            P(AXES, None, None),
        ),
        out_specs=P(AXES, None),
        check_vma=False,
    )
```

```python
import math

import jax
import jax.numpy as jnp
from jax import lax
from jax.experimental import pallas as pl
from jax.experimental.pallas import tpu as pltpu
from jax.sharding import PartitionSpec as P

FF = 1024
LANES = 128
SMALL_VMEM = 2 << 20
MLP_VMEM = 8 << 20
MLP_TILE = 1024
PREFETCH_WINDOW = pl.CostEstimate(flops=64 << 30, transcendentals=0, bytes_accessed=256 << 20)
AXES = ("grp", "fsdp")


def device_index():
    return lax.axis_index("grp") * lax.axis_size("fsdp") + lax.axis_index("fsdp")


def rms_normed(tokens, norm_gain):
    as_float = tokens.astype(jnp.float32)
    mean_square = jnp.mean(as_float * as_float, axis=-1, keepdims=True)
    return (as_float * lax.rsqrt(mean_square + 1e-06) * norm_gain).astype(jnp.bfloat16)


def expert_mlp(rows, w_gate_up, w_down):
    hidden_dev = w_down.shape[1]
    projected = jnp.dot(rows, w_gate_up[0], preferred_element_type=jnp.float32)
    hidden = (jax.nn.silu(projected[:, :hidden_dev]) * projected[:, hidden_dev:]).astype(
        jnp.bfloat16
    )
    return jnp.dot(hidden, w_down[0], preferred_element_type=jnp.float32).astype(jnp.bfloat16)


def row_payload(tokens, norm_gain, routes, gate_probs):
    rows_dev, width = tokens.shape
    top_count = routes.shape[1]
    total = width + LANES * -(-2 * top_count // LANES)

    def kernel(*refs):
        sources, payload_ref, targets, sems = refs[:4], refs[4], refs[5:9], refs[9]
        copies = [
            pltpu.make_async_copy(source, target, sems.at[index])
            for index, (source, target) in enumerate(zip(sources, targets))
        ]
        for copy in copies:
            copy.start()
        for copy in copies:
            copy.wait()
        tokens_ref, gain_ref, routes_ref, probs_ref = targets
        as_float = tokens_ref[...].astype(jnp.float32)
        mean_square = jnp.mean(as_float * as_float, axis=-1, keepdims=True)
        scaled = as_float * lax.rsqrt(mean_square + 1e-06) * gain_ref[...]
        payload_ref[:, :width] = scaled.astype(jnp.bfloat16)
        control = jnp.concatenate(
            [
                routes_ref[...].astype(jnp.float32),
                probs_ref[...].astype(jnp.float32),
                jnp.zeros((rows_dev, total - width - 2 * top_count), jnp.float32),
            ],
            axis=1,
        )
        payload_ref[:, width:] = control.astype(jnp.bfloat16)

    operands = (tokens, norm_gain.reshape(1, width), routes, gate_probs)
    return pl.pallas_call(
        kernel,
        out_shape=jax.ShapeDtypeStruct((rows_dev, total), jnp.bfloat16),
        in_specs=[pl.BlockSpec(memory_space=pltpu.HBM)] * 4,
        out_specs=pl.BlockSpec(memory_space=pltpu.VMEM),
        scratch_shapes=[pltpu.VMEM(o.shape, o.dtype) for o in operands]
        + [pltpu.SemaphoreType.DMA((4,))],
        compiler_params=pltpu.CompilerParams(vmem_limit_bytes=SMALL_VMEM),
        name="row_payload",
    )(*[pltpu.with_memory_space_constraint(o, pltpu.HBM) for o in operands])


def stacked(pieces):
    def kernel(*refs):
        for index, ref in enumerate(refs[:-1]):
            refs[-1][index] = ref[...]

    vmem = pl.BlockSpec(memory_space=pltpu.VMEM)
    return pl.pallas_call(
        kernel,
        out_shape=jax.ShapeDtypeStruct((len(pieces),) + pieces[0].shape, pieces[0].dtype),
        in_specs=[vmem] * len(pieces),
        out_specs=vmem,
        compiler_params=pltpu.CompilerParams(vmem_limit_bytes=SMALL_VMEM),
        cost_estimate=PREFETCH_WINDOW,
        name="stacked",
    )(*pieces)


def weighted_parts(own, other, gate_up_pieces, w_down, top_count):
    hidden_dev, width = w_down.shape
    blocks = list(own) + list(other)
    block_rows = blocks[0].shape[0] * blocks[0].shape[1]
    total = blocks[0].shape[2]
    row_count = block_rows * len(blocks)
    half = width // 2
    piece_count = len(gate_up_pieces)
    tile = math.gcd(math.gcd(hidden_dev, half), MLP_TILE)
    out_block = (row_count // blocks[0].shape[1], blocks[0].shape[1], half)

    def projected(rows_ref, piece_refs, column):
        sum_so_far, first = None, 0
        for piece in piece_refs:
            last = first + piece.shape[0]
            term = jnp.dot(
                rows_ref[:, first:last],
                piece[:, pl.ds(column, tile)],
                preferred_element_type=jnp.float32,
            )
            sum_so_far, first = term if sum_so_far is None else sum_so_far + term, last
        return sum_so_far

    def kernel(*refs):
        my_expert = device_index() // (FF // hidden_dev)
        block_refs, refs = refs[: len(blocks)], refs[len(blocks) :]
        piece_refs, refs = refs[:piece_count], refs[piece_count:]
        down_ref, other_out, hidden_ref, weight_out, rows_ref = refs
        core = lax.rem(lax.axis_index("fsdp"), 2)
        for index, source in enumerate(block_refs):
            rows_ref[index * block_rows : (index + 1) * block_rows, :] = source[...].reshape(
                block_rows, total
            )
        control = rows_ref[:, width:].astype(jnp.float32)
        sent_routes = control[:, :top_count].astype(jnp.int32)
        probs = control[:, top_count : 2 * top_count]
        combine = probs / jnp.sum(probs, axis=-1, keepdims=True)
        row_weight = jnp.sum(
            jnp.where(sent_routes == my_expert, combine, 0.0), axis=-1, keepdims=True
        )
        for column in range(0, hidden_dev, tile):
            gate = projected(rows_ref, piece_refs, column)
            up = projected(rows_ref, piece_refs, hidden_dev + column)
            hidden_ref[:, column : column + tile] = (jax.nn.silu(gate) * up).astype(jnp.bfloat16)
        weight_out[...] = jnp.broadcast_to(row_weight, weight_out.shape)
        weighted_columns(hidden_ref, down_ref, (1 - core) * half, row_weight, other_out, tile)

    vmem = pl.BlockSpec(memory_space=pltpu.VMEM)
    return pl.pallas_call(
        kernel,
        out_shape=[
            jax.ShapeDtypeStruct(out_block, jnp.bfloat16),
            jax.ShapeDtypeStruct((row_count, hidden_dev), jnp.bfloat16),
            jax.ShapeDtypeStruct((row_count, LANES), jnp.float32),
        ],
        in_specs=[vmem] * (len(blocks) + piece_count + 1),
        out_specs=[vmem] * 3,
        scratch_shapes=[
            pltpu.VMEM((row_count, total), jnp.bfloat16),
        ],
        compiler_params=pltpu.CompilerParams(vmem_limit_bytes=MLP_VMEM),
        name="weighted_parts",
    )(
        *blocks,
        *[pltpu.with_memory_space_constraint(piece, pltpu.VMEM) for piece in gate_up_pieces],
        pltpu.with_memory_space_constraint(w_down, pltpu.VMEM),
    )


def weighted_columns(hidden_ref, down_ref, first, row_weight, out, tile):
    for column in range(0, out.shape[2], tile):
        columns = slice(column, column + tile)
        source = pl.ds(pl.multiple_of(first + column, tile), tile)
        part = jnp.dot(hidden_ref[...], down_ref[:, source], preferred_element_type=jnp.float32)
        weighted = part.astype(jnp.bfloat16).astype(jnp.float32) * row_weight
        out[:, :, columns] = weighted.reshape(out.shape[:2] + (tile,)).astype(out.dtype)


def own_columns(hidden, weight, w_down, out_block):
    tile = math.gcd(out_block[2], MLP_TILE)

    def kernel(hidden_ref, weight_ref, down_ref, out):
        first = lax.rem(lax.axis_index("fsdp"), 2) * out_block[2]
        weighted_columns(hidden_ref, down_ref, first, weight_ref[:, :1], out, tile)

    vmem = pl.BlockSpec(memory_space=pltpu.VMEM)
    return pl.pallas_call(
        kernel,
        out_shape=jax.ShapeDtypeStruct(out_block, jnp.float32),
        in_specs=[vmem] * 3,
        out_specs=vmem,
        compiler_params=pltpu.CompilerParams(vmem_limit_bytes=MLP_VMEM),
        cost_estimate=pl.CostEstimate(
            flops=hidden.shape[0] * w_down.size, transcendentals=0, bytes_accessed=w_down.nbytes // 2
        ),
        name="own_columns",
    )(hidden, weight, pltpu.with_memory_space_constraint(w_down, pltpu.VMEM))


def chip_sum(own_part, partner_part):
    pair_count = own_part.shape[0] // 2

    def kernel(own_ref, partner_ref, sum_ref):
        me = device_index()
        core = lax.rem(me, 2)
        for chip in range(pair_count):
            same = jnp.bitwise_xor(me // 2, chip)
            flip = pair_count + same
            for mine, theirs, place in ((same, flip, core), (flip, same, 1 - core)):
                total = own_ref[mine] + partner_ref[theirs].astype(jnp.float32)
                sum_ref[2 * chip + place] = total.astype(jnp.bfloat16)

    vmem = pl.BlockSpec(memory_space=pltpu.VMEM)
    return pl.pallas_call(
        kernel,
        out_shape=jax.ShapeDtypeStruct(own_part.shape, jnp.bfloat16),
        in_specs=[vmem] * 2,
        out_specs=vmem,
        compiler_params=pltpu.CompilerParams(vmem_limit_bytes=SMALL_VMEM),
        name="chip_sum",
    )(own_part, partner_part)


def row_sum(returned):
    device_count, rows_dev, half = returned.shape

    def kernel(returned_ref, out_ref):
        for core in range(2):
            total = returned_ref[core].astype(jnp.float32)
            for device in range(core + 2, device_count, 2):
                total += returned_ref[device].astype(jnp.float32)
            out_ref[:, core * half : (core + 1) * half] = total.astype(jnp.bfloat16)

    vmem = pl.BlockSpec(memory_space=pltpu.VMEM)
    return pl.pallas_call(
        kernel,
        out_shape=jax.ShapeDtypeStruct((rows_dev, 2 * half), jnp.bfloat16),
        in_specs=[vmem],
        out_specs=vmem,
        compiler_params=pltpu.CompilerParams(vmem_limit_bytes=SMALL_VMEM),
        name="row_sum",
    )(returned)


def exchanged(value, axis, flip):
    size = lax.axis_size(axis)
    return lax.ppermute(value, axis, [(d, d ^ flip) for d in range(size)])


def every_row(tokens, norm_gain, routes, gate_probs, w_gate_up, w_down):
    shard_count = lax.axis_size("fsdp")
    group_count = lax.axis_size("grp")

    payload = row_payload(tokens, norm_gain, routes, gate_probs)
    column = [payload] + [exchanged(payload, "fsdp", k) for k in range(2, shard_count, 2)]
    column = stacked(column)
    plane = [exchanged(column, "grp", k) for k in range(1, group_count)]
    own = [column] + plane
    other = [exchanged(block, "fsdp", 1) for block in own]
    other_part, hidden, weight = weighted_parts(own, other, [w_gate_up[0]], w_down[0], routes.shape[1])
    from_partner = exchanged(other_part, "fsdp", 1)
    own_part = own_columns(hidden, weight, w_down[0], other_part.shape)
    summed = chip_sum(own_part, from_partner)
    return row_sum(lax.all_to_all(summed, AXES, 0, 0, tiled=True))


def routed_rows(tokens, norm_gain, routes, gate_probs, w_gate_up, w_down):
    group_count = lax.axis_size("grp")
    shard_count = lax.axis_size("fsdp")
    shard_index = lax.axis_index("fsdp")
    split_count = FF // w_down.shape[1]
    rows_dev, width = tokens.shape
    block_rows = rows_dev * shard_count
    capacity = slot_capacity(tokens, routes, w_down)
    normed = rms_normed(tokens, norm_gain)
    rows_all = lax.all_gather(normed, "fsdp", axis=0, tiled=True)
    probs_all = lax.all_gather(gate_probs, "fsdp", axis=0, tiled=True)
    routes_all = lax.all_gather(routes, "fsdp", axis=0, tiled=True)
    probs = probs_all.astype(jnp.float32)
    combine = probs / jnp.sum(probs, axis=-1, keepdims=True)
    targets = (
        jnp.arange(group_count, dtype=jnp.int32) * (shard_count // split_count)
        + shard_index // split_count
    )
    matched = routes_all[None, :, :] == targets[:, None, None]
    is_routed = jnp.any(matched, axis=-1)
    row_weight = jnp.sum(jnp.where(matched, combine[None, :, :], 0.0), axis=-1)
    row_ids = jnp.arange(block_rows, dtype=jnp.int32)
    earlier = row_ids[:, None] >= row_ids[None, :]
    slot_index = jnp.sum(is_routed[:, None, :] & earlier[None], axis=-1, dtype=jnp.int32) - 1
    select = (
        slot_index[:, None, :] == jnp.arange(capacity, dtype=jnp.int32)[None, :, None]
    ) & is_routed[:, None, :]
    outgoing = jnp.einsum(
        "gcb,bd->gcd", select.astype(jnp.bfloat16), rows_all, preferred_element_type=jnp.float32
    ).astype(jnp.bfloat16)
    incoming = lax.all_to_all(outgoing, "grp", split_axis=0, concat_axis=0, tiled=True)
    result = expert_mlp(incoming.reshape(-1, width), w_gate_up, w_down)
    returned = lax.all_to_all(
        result.reshape(incoming.shape), "grp", split_axis=0, concat_axis=0, tiled=True
    )
    mix_matrix = (select.astype(jnp.float32) * row_weight[:, None, :]).reshape(-1, block_rows)
    row_partial = jnp.dot(
        mix_matrix.T,
        returned.reshape(-1, width),
        precision=lax.Precision.HIGHEST,
        preferred_element_type=jnp.float32,
    )
    summed = lax.psum_scatter(row_partial, "fsdp", scatter_dimension=0, tiled=True)
    return summed.astype(jnp.bfloat16)


def slot_capacity(tokens, routes, w_down):
    block_rows = tokens.shape[0] * lax.axis_size("fsdp")
    expert_count = lax.axis_size(AXES) * w_down.shape[1] // FF
    return 2 * block_rows * routes.shape[1] // expert_count


def local(tokens, norm_gain, routes, gate_probs, w_gate_up, w_down):
    block_rows = tokens.shape[0] * lax.axis_size("fsdp")
    dense = block_rows <= 2 * slot_capacity(tokens, routes, w_down)
    paired = lax.axis_size("fsdp") > 1 and lax.axis_size(AXES) & (lax.axis_size(AXES) - 1) == 0
    plan = every_row if dense and paired else routed_rows
    return plan(tokens, norm_gain, routes, gate_probs, w_gate_up, w_down)


def solution(mesh):
    return jax.shard_map(
        local,
        mesh=mesh,
        in_specs=(
            P(AXES, None),
            P(),
            P(AXES, None),
            P(AXES, None),
            P(AXES, None, None),
            P(AXES, None, None),
        ),
        out_specs=P(AXES, None),
        check_vma=False,
    )
```
